256 devices in a mesh: dp: 16 (over y_lo, x, core), fsdp: 16 (over z, y_hi).
Axes of the slice: x: 4, y: 4 (y_hi: 2, y_lo: 2; y = y_hi * 2 + y_lo), z: 8, core: 2. Of those that a mesh axis runs over, the one named last changes fastest.
Arguments:
- img_emb: bfloat16 [8192, 1024], P(('dp', 'fsdp')), may hold values from -0.25 to 0.25
- txt_emb: bfloat16 [8192, 1024], P(('dp', 'fsdp')), may hold values from -0.25 to 0.25
- img_ids: int32 [8192], P(('dp', 'fsdp')), may hold values from 0 to 8191
- txt_ids: int32 [8192], P(('dp', 'fsdp')), may hold values from 0 to 8191
- temp_log: float32 [1], replicated, may hold values from 1.5 to 2.5
- logit_bias: float32 [1], replicated, may hold values from -6 to -2
- block_in: bfloat16 [16384, 3072], P(('dp', 'fsdp')), may hold values from -6 to 6
- dw_kernel: float32 [49, 3072], replicated, may hold values from -0.875 to 0.875
- ln_gain: float32 [3072], replicated, may hold values from 0.5 to 1.5
- ln_bias: float32 [3072], replicated, may hold values from -3 to 3
- w_up: bfloat16 [3072, 6144], P(None, 'fsdp'), may hold values from -0.109375 to 0.109375
- w_down: bfloat16 [6144, 3072], P('fsdp'), may hold values from -0.078125 to 0.078125
- layer_scale: float32 [3072], replicated, may hold values from 0.1 to 1
- head_gain: float32 [3072], replicated, may hold values from 0.5 to 1.5
- head_bias: float32 [3072], replicated, may hold values from -3 to 3
- w_proj: bfloat16 [3072, 1024], replicated, may hold values from -0.109375 to 0.109375
Outputs:
- img_grad: float32 [8192, 1024], P(('dp', 'fsdp'))
- txt_grad: float32 [8192, 1024], P(('dp', 'fsdp'))
- w_up_grad: float32 [3072, 6144], P('dp', 'fsdp')
- w_down_grad: float32 [6144, 3072], P('fsdp', 'dp')
The draws below stay inside these ranges and needn't reach their ends.
All inputs are finite; a program needn't handle non-finite values.
Results may differ from the reference program's by a relative error of at most 0.02.
Values may be sent and summed in bfloat16 or wider, within the bound.
No kernel may reach another device: no remote copies, remote signals or barrier semaphores. Data moves between devices by JAX's collectives and lax.ppermute only.
A program may use at most 128 MiB of HBM per device.

```python
import math
import jax
import jax.numpy as jnp
from jax import lax

WIDTH = 3072
HIDDEN_SIZE = 6144
EMBED = 1024
KERNEL = 7
SIDE = 8
PAIR_DEV = 32
PAIRS = 8192
IMAGE_ROWS = 16384
N_DP = 16
N_FSDP = 16


def set_ends(result, rng, least, top_value):
    shape = result.shape
    spot = [jax.random.randint(jax.random.fold_in(rng, axis), (), 0, shape[axis]) for axis in range(len(shape))]
    result = result.at[tuple(spot)].set(least)
    longest = shape.index(max(shape))
    spot[longest] = (spot[longest] + 1) % shape[longest]
    return result.at[tuple(spot)].set(top_value)


def block_levels(rng, dims, pieces, low, top_value):
    gain, own = 1.0, jax.random.fold_in(rng, 6)
    for dim, blocks in pieces:
        heights = jnp.exp(jax.random.uniform(jax.random.fold_in(own, dim), (blocks,), jnp.float32, low / len(pieces), top_value / len(pieces)))
        gain = gain * jnp.repeat(heights, dims[dim] // blocks).reshape([-1 if axis == dim else 1 for axis in range(len(dims))])
    return gain


def scatter_about(rng, dims, deviation, limit, cuts=(), held_as=jnp.bfloat16):
    values = deviation * jax.random.normal(rng, dims, jnp.float32)
    if cuts:
        values = values * block_levels(rng, dims, cuts, -0.22, 0.18)
    return jnp.clip(values, -limit, limit).astype(held_as)


def setup_inputs(seed: int = 0) -> dict:
    seeds = jax.random.split(jax.random.key(seed), 17)
    return {
        "img_emb": scatter_about(seeds[0], (PAIRS, EMBED), 0.03125, 0.25, ((0, 256),)),
        "txt_emb": scatter_about(seeds[1], (PAIRS, EMBED), 0.03125, 0.25, ((0, 256),)),
        "img_ids": set_ends(jax.random.randint(seeds[2], (PAIRS,), 0, PAIRS), jax.random.fold_in(seeds[2], 1), 0, PAIRS - 1).astype(jnp.int32),
        "txt_ids": set_ends(jax.random.randint(seeds[3], (PAIRS,), 0, PAIRS), jax.random.fold_in(seeds[3], 1), 0, PAIRS - 1).astype(jnp.int32),
        "temp_log": jnp.clip(jax.random.uniform(seeds[4], (1,), jnp.float32, 1.5, 2.5), 1.5, 2.5),
        "logit_bias": jnp.clip(jax.random.uniform(seeds[5], (1,), jnp.float32, -6.0, -2.0), -6.0, -2.0),
        "block_in": scatter_about(seeds[6], (IMAGE_ROWS, WIDTH), 1.0, 6.0, ((0, 256),)),
        "dw_kernel": scatter_about(seeds[7], (KERNEL * KERNEL, WIDTH), (KERNEL * KERNEL) ** -0.5, 0.875, (), jnp.float32),
        "ln_gain": jnp.clip(1.0 + 0.1 * jax.random.normal(seeds[8], (WIDTH,), jnp.float32), 0.5, 1.5),
        "ln_bias": scatter_about(seeds[9], (WIDTH,), 0.5, 3.0, (), jnp.float32),
        "w_up": scatter_about(seeds[10], (WIDTH, HIDDEN_SIZE), WIDTH ** -0.5, 0.109375, ((1, 16),)),
        "w_down": scatter_about(seeds[11], (HIDDEN_SIZE, WIDTH), HIDDEN_SIZE ** -0.5, 0.078125, ((0, 16),)),
        "layer_scale": jnp.clip(jnp.exp(jax.random.uniform(seeds[12], (WIDTH,), jnp.float32, math.log(0.1), math.log(1.0))), 0.1, 1.0),
        "head_gain": jnp.clip(1.0 + 0.1 * jax.random.normal(seeds[13], (WIDTH,), jnp.float32), 0.5, 1.5),
        "head_bias": scatter_about(seeds[14], (WIDTH,), 0.5, 3.0, (), jnp.float32),
        "w_proj": scatter_about(seeds[15], (WIDTH, EMBED), WIDTH ** -0.5, 0.109375),
    }


def unit_rows(matrix):
    values = matrix.astype(jnp.float32)
    length = jnp.sqrt(lax.optimization_barrier(jnp.sum(values * values, axis=1, keepdims=True)) + 1e-06)
    return (values / length, length)

def back_unit(gradient, unit_part, length):
    inner_prod = lax.optimization_barrier(jnp.sum(unit_part * gradient, axis=1, keepdims=True))
    return (gradient - unit_part * inner_prod) / length

def pair_tile(images, image_ids, text_rows, text_ids, temper, offset):
    scores = jnp.dot(images, text_rows.T, preferred_element_type=jnp.float32)
    logits = temper * scores + offset
    labels = jnp.where(image_ids[:, None] == text_ids[None, :], 1.0, -1.0)
    weights = (temper * -labels * jax.nn.sigmoid(-labels * logits)).astype(jnp.bfloat16)
    image_part = jnp.dot(weights, text_rows, preferred_element_type=jnp.float32)
    text_part = jnp.dot(weights.T, images, preferred_element_type=jnp.float32)
    return (image_part, text_part)

def depthwise(pictures, kernel):
    reach = KERNEL // 2
    padded = jnp.pad(pictures, ((0, 0), (reach, reach), (reach, reach), (0, 0)))
    summed = jnp.zeros_like(pictures)
    for above in range(KERNEL):
        for across in range(KERNEL):
            summed = summed + kernel[above * KERNEL + across] * padded[:, above:above + SIDE, across:across + SIDE, :]
    return summed

def layer_norm(values, gain_vec, bias_vec):
    centre = lax.optimization_barrier(jnp.mean(values, axis=-1, keepdims=True))
    centred = values - centre
    inverse = 1.0 / jnp.sqrt(lax.optimization_barrier(jnp.mean(centred * centred, axis=-1, keepdims=True)) + 1e-06)
    normal = centred * inverse
    return (normal * gain_vec + bias_vec, normal, inverse)

def head_back(patch_means, block_mean, image_sum, layer_scale, head_gain, head_bias, w_proj):
    pooled = patch_means.astype(jnp.float32) + layer_scale * block_mean
    head_out, head_norm, inverse = layer_norm(pooled, head_gain, head_bias)
    embed = jnp.dot(head_out.astype(jnp.bfloat16), w_proj, preferred_element_type=jnp.float32)
    embed_unit, embed_len = unit_rows(embed)
    embed_grad = back_unit(image_sum, embed_unit, embed_len).astype(jnp.bfloat16)
    head_grad = jnp.dot(embed_grad, w_proj.T, preferred_element_type=jnp.float32)
    norm_grad = head_grad * head_gain
    pool_grad = inverse * (norm_grad - lax.optimization_barrier(jnp.mean(norm_grad, axis=1, keepdims=True)) - head_norm * lax.optimization_barrier(jnp.mean(norm_grad * head_norm, axis=1, keepdims=True)))
    return (layer_scale * pool_grad / (SIDE * SIDE)).astype(jnp.bfloat16)

def reference(img_emb, txt_emb, img_ids, txt_ids, temp_log, logit_bias, block_in, dw_kernel, ln_gain, ln_bias, w_up, w_down, layer_scale, head_gain, head_bias, w_proj):
    temper = jnp.exp(temp_log[0])
    offset = logit_bias[0]
    img_unit, img_len = unit_rows(img_emb)
    txt_unit, txt_len = unit_rows(txt_emb)
    img_b = img_unit.astype(jnp.bfloat16)
    txt_b = txt_unit.astype(jnp.bfloat16)
    group_rows = N_FSDP * PAIR_DEV
    col_rows = N_DP * PAIR_DEV
    txt_cols = txt_b.reshape(N_DP, N_FSDP, PAIR_DEV, EMBED)
    id_cols = txt_ids.reshape(N_DP, N_FSDP, PAIR_DEV)

    def tile(running, tile_no):
        img_tot, txt_tot = running
        group_no = tile_no // N_FSDP
        column_no = tile_no % N_FSDP
        images = lax.dynamic_slice_in_dim(img_b, group_no * group_rows, group_rows, 0)
        image_ids = lax.dynamic_slice_in_dim(img_ids, group_no * group_rows, group_rows, 0)
        text_rows = lax.dynamic_index_in_dim(txt_cols, column_no, 1, keepdims=False).reshape(col_rows, EMBED)
        text_ids = lax.dynamic_index_in_dim(id_cols, column_no, 1, keepdims=False).reshape(col_rows)
        image_part, text_part = pair_tile(images, image_ids, text_rows, text_ids, temper, offset)
        image_part = lax.optimization_barrier(image_part.astype(jnp.bfloat16)).astype(jnp.float32)
        text_part = lax.optimization_barrier(text_part.astype(jnp.bfloat16)).astype(jnp.float32)
        return ((img_tot.at[group_no].add(image_part), txt_tot.at[column_no].add(text_part)), None)
    start = (jnp.zeros((N_DP, group_rows, EMBED), jnp.float32), jnp.zeros((N_FSDP, col_rows, EMBED), jnp.float32))
    (img_tot, txt_tot), _ = lax.scan(tile, start, jnp.arange(N_DP * N_FSDP, dtype=jnp.int32))
    img_sum = img_tot.reshape(PAIRS, EMBED)
    txt_sum = jnp.transpose(txt_tot.reshape(N_FSDP, N_DP, PAIR_DEV, EMBED), (1, 0, 2, 3)).reshape(PAIRS, EMBED)
    img_grad = back_unit(img_sum, img_unit, img_len)
    txt_grad = back_unit(txt_sum, txt_unit, txt_len)
    patch_rows = N_FSDP * SIDE * SIDE
    down_wide = w_down.astype(jnp.float32)

    def group_step(running, group_no):
        up_tot, down_tot = running
        patches = lax.dynamic_slice_in_dim(block_in, group_no * patch_rows, patch_rows, 0).astype(jnp.float32)
        pictures = patches.reshape(N_FSDP, SIDE, SIDE, WIDTH)
        mixed_rows = depthwise(pictures, dw_kernel).reshape(patch_rows, WIDTH)
        normed = layer_norm(mixed_rows, ln_gain, ln_bias)[0].astype(jnp.bfloat16)
        hidden = jnp.dot(normed, w_up, preferred_element_type=jnp.float32)
        active = jax.nn.gelu(hidden).astype(jnp.bfloat16)
        active_mean = lax.optimization_barrier(jnp.mean(active.astype(jnp.float32).reshape(N_FSDP, SIDE * SIDE, HIDDEN_SIZE), axis=1))
        block_mean = jnp.dot(active_mean, down_wide, precision=lax.Precision.HIGHEST)
        patch_means = lax.optimization_barrier(jnp.mean(pictures, axis=(1, 2))).astype(jnp.bfloat16)
        group_sum = lax.dynamic_slice_in_dim(img_sum, group_no * group_rows, group_rows, 0)
        micro_sum = group_sum.reshape(N_FSDP, PAIR_DEV, EMBED)[:, 0]
        grad_row = head_back(patch_means, block_mean, micro_sum, layer_scale, head_gain, head_bias, w_proj)
        out_grad = jnp.broadcast_to(grad_row[:, None, :], (N_FSDP, SIDE * SIDE, WIDTH)).reshape(patch_rows, WIDTH)
        down_grad = jnp.dot(out_grad, w_down.T, preferred_element_type=jnp.float32)
        _, pullback = jax.vjp(jax.nn.gelu, hidden)
        hid_grad = pullback(down_grad)[0].astype(jnp.bfloat16)
        down_part = jnp.dot(active.T, out_grad, preferred_element_type=jnp.float32)
        up_part = jnp.dot(normed.T, hid_grad, preferred_element_type=jnp.float32)
        up_tot = up_tot + lax.optimization_barrier(up_part.astype(jnp.bfloat16)).astype(jnp.float32)
        down_tot = down_tot + lax.optimization_barrier(down_part.astype(jnp.bfloat16)).astype(jnp.float32)
        return ((up_tot, down_tot), None)
    start = (jnp.zeros((WIDTH, HIDDEN_SIZE), jnp.float32), jnp.zeros((HIDDEN_SIZE, WIDTH), jnp.float32))
    (w_up_grad, w_down_grad), _ = lax.scan(group_step, start, jnp.arange(N_DP, dtype=jnp.int32))
    return (img_grad, txt_grad, w_up_grad, w_down_grad)
```

```python
import jax
import jax.numpy as jnp
from jax import lax
from jax.sharding import Mesh
from jax.sharding import PartitionSpec as P

KERNEL = 7
SIDE = 8
PATCHES = SIDE * SIDE
DP = ("ylo", "x", "core")
FSDP = ("z", "yhi")
ALL = DP + FSDP
NZ = 8
BF = jnp.bfloat16
F32 = jnp.float32


def hop(value, axis, length, step):
    return lax.ppermute(value, axis, [(i, (i + step) % length) for i in range(length)])


def ring_blocks(block):
    other = hop(block, "yhi", 2, 1)
    got = {(0, 0): block, (0, 1): other}
    order = [(0, 0), (0, 1)]
    up = [block, other]
    down = [block, other]
    for step in range(1, NZ // 2 + 1):
        last = step == NZ // 2
        for side in range(2):
            if not last or side == 0:
                up[side] = hop(up[side], "z", NZ, 1)
                got[(NZ - step) % NZ, side] = up[side]
                order.append(((NZ - step) % NZ, side))
            if not last or side == 1:
                down[side] = hop(down[side], "z", NZ, -1)
                got[step % NZ, side] = down[side]
                order.append((step % NZ, side))
    return got, order


def to_absolute(stacked):
    z = lax.axis_index("z")
    y = lax.axis_index("yhi")
    rolled = jnp.roll(stacked, z, axis=0)
    turned = jnp.where(y == 0, rolled, rolled[:, ::-1])
    return turned.reshape(16, *stacked.shape[2:])


def to_relative(whole):
    z = lax.axis_index("z")
    y = lax.axis_index("yhi")
    parts = whole.reshape(NZ, 2, *whole.shape[1:])
    turned = jnp.where(y == 0, parts, parts[:, ::-1])
    return jnp.roll(turned, -z, axis=0)


def unit_rows(matrix):
    values = matrix.astype(F32)
    length = jnp.sqrt(jnp.sum(values * values, axis=1, keepdims=True) + 1e-06)
    return (values / length, length)


def back_unit(gradient, unit_part, length):
    inner_prod = jnp.sum(unit_part * gradient, axis=1, keepdims=True)
    return (gradient - unit_part * inner_prod) / length


def with_ids(rows, ids):
    digits = jnp.stack([ids // 128, ids % 128], axis=1).astype(BF)
    return jnp.concatenate([rows, jnp.pad(digits, ((0, 0), (0, 126)))], axis=1)


def ids_of(payload):
    width = payload.shape[1] - 128
    return payload[:, width].astype(F32) * 128.0 + payload[:, width + 1].astype(F32)


def depthwise(pictures, kernel):
    reach = KERNEL // 2
    padded = jnp.pad(pictures, ((0, 0), (reach, reach), (reach, reach), (0, 0)))
    summed = jnp.zeros_like(pictures)
    for above in range(KERNEL):
        for across in range(KERNEL):
            summed = (
                summed
                + kernel[above * KERNEL + across]
                * padded[:, above : above + SIDE, across : across + SIDE, :]
            )
    return summed


def layer_norm(values, gain_vec, bias_vec):
    centre = jnp.mean(values, axis=-1, keepdims=True)
    centred = values - centre
    inverse = 1.0 / jnp.sqrt(jnp.mean(centred * centred, axis=-1, keepdims=True) + 1e-06)
    normal = centred * inverse
    return (normal * gain_vec + bias_vec, normal, inverse)


def head_back(patch_means, block_mean, image_sum, layer_scale, head_gain, head_bias, w_proj):
    pooled = patch_means.astype(F32) + layer_scale * block_mean
    head_out, head_norm, inverse = layer_norm(pooled, head_gain, head_bias)
    embed = jnp.dot(head_out.astype(BF), w_proj, preferred_element_type=F32)
    embed_unit, embed_len = unit_rows(embed)
    embed_grad = back_unit(image_sum, embed_unit, embed_len).astype(BF)
    head_grad = jnp.dot(embed_grad, w_proj.T, preferred_element_type=F32)
    norm_grad = head_grad * head_gain
    pool_grad = inverse * (
        norm_grad
        - jnp.mean(norm_grad, axis=1, keepdims=True)
        - head_norm * jnp.mean(norm_grad * head_norm, axis=1, keepdims=True)
    )
    return (layer_scale * pool_grad / PATCHES).astype(BF)


def on_device(
    img_emb,
    txt_emb,
    img_ids,
    txt_ids,
    temp_log,
    logit_bias,
    block_in,
    dw_kernel,
    ln_gain,
    ln_bias,
    w_up,
    w_down,
    layer_scale,
    head_gain,
    head_bias,
    w_proj,
):
    channels = block_in.shape[1]
    hid_width = w_up.shape[1]
    pairs, width = img_emb.shape
    temper = jnp.exp(temp_log[0])
    offset = logit_bias[0]
    img_unit, img_len = unit_rows(img_emb)
    txt_unit, txt_len = unit_rows(txt_emb)
    img_pay = with_ids(img_unit.astype(BF), img_ids)
    txt_pay = with_ids(txt_unit.astype(BF), txt_ids)

    img_got, img_order = ring_blocks(img_pay)
    texts = lax.all_to_all(
        jnp.broadcast_to(txt_pay[None], (16, *txt_pay.shape)), DP, 0, 0, tiled=True
    ).reshape(16 * pairs, -1)

    pictures = block_in.astype(F32).reshape(1, SIDE, SIDE, channels)
    mixed_rows = depthwise(pictures, dw_kernel).reshape(PATCHES, channels)
    normed = layer_norm(mixed_rows, ln_gain, ln_bias)[0].astype(BF)
    patch_means = jnp.mean(pictures, axis=(1, 2)).astype(BF)
    got, order = ring_blocks(normed)

    keys = [(s, t) for s in range(NZ) for t in range(2)]
    images = jnp.concatenate([img_got[k] for k in keys], axis=0)
    image_ids = ids_of(images)
    text_ids = ids_of(texts)
    images = images[:, :width]
    text_rows = texts[:, :width]
    scores = jnp.dot(images, text_rows.T, preferred_element_type=F32)
    logits = temper * scores + offset
    labels = jnp.where(image_ids[:, None] == text_ids[None, :], 1.0, -1.0)
    weights = (temper * -labels * jax.nn.sigmoid(-labels * logits)).astype(BF)
    image_part = jnp.dot(weights, text_rows, preferred_element_type=F32).astype(BF)
    text_part = jnp.dot(weights.T, images, preferred_element_type=F32).astype(BF)
    image_rel = image_part.reshape(NZ, 2, pairs, width)

    text_sum = jnp.sum(
        lax.all_to_all(text_part.reshape(16, pairs, width), DP, 0, 0, tiled=True).astype(F32),
        axis=0,
    )

    hidden, totals = {}, {}
    for k in order:
        hidden[k] = jnp.dot(got[k], w_up, preferred_element_type=F32)
        active = jax.nn.gelu(hidden[k]).astype(BF)
        totals[k] = jnp.sum(active.astype(F32), axis=0)
    active_total = jnp.stack([totals[k] for k in keys])
    mean = active_total / PATCHES
    first = lax.reduce_precision(mean, 8, 7)
    rest = mean - first
    second = lax.reduce_precision(rest, 8, 7)
    third = lax.reduce_precision(rest - second, 8, 7)
    three = jnp.concatenate([first, second, third], axis=0).astype(BF)
    partial = jnp.sum(
        jnp.dot(three, w_down, preferred_element_type=F32).reshape(3, 16, channels), axis=0
    )
    mine = jnp.concatenate(
        [partial.astype(BF).reshape(NZ, 2, channels), image_rel[:, :, 0, :]], axis=2
    )
    summed = jnp.sum(
        lax.all_to_all(to_absolute(mine).reshape(16, 1, -1), FSDP, 0, 0, tiled=True).astype(F32),
        axis=0,
    )
    grad_row = head_back(
        patch_means,
        summed[:, :channels],
        summed[:, channels:],
        layer_scale,
        head_gain,
        head_bias,
        w_proj,
    )
    group_grad = lax.all_to_all(
        jnp.broadcast_to(grad_row[None], (16, 1, channels)), FSDP, 0, 0, tiled=True
    ).reshape(16, channels)

    image_sum = jnp.sum(
        lax.all_to_all(to_absolute(image_rel), FSDP, 0, 0, tiled=True).astype(F32), axis=0
    )

    grads_rel = to_relative(group_grad).reshape(16, channels)
    row_down = jnp.dot(grads_rel, w_down.T, preferred_element_type=F32)
    whole_hidden = jnp.concatenate([hidden[k] for k in keys], axis=0)
    whole_normed = jnp.concatenate([got[k] for k in keys], axis=0)
    down_grad = jnp.broadcast_to(row_down[:, None, :], (16, PATCHES, hid_width)).reshape(
        -1, hid_width
    )
    _, pullback = jax.vjp(jax.nn.gelu, whole_hidden)
    hid_grad = pullback(down_grad)[0].astype(BF)
    up_part = jnp.dot(whole_normed.T, hid_grad, preferred_element_type=F32).astype(BF)
    up_part = up_part.reshape(8, 2, channels // 16, hid_width)
    core = lax.axis_index("core")
    keep = lax.dynamic_index_in_dim(up_part, core, 1, keepdims=False)
    send = lax.dynamic_index_in_dim(up_part, 1 - core, 1, keepdims=False)
    both = (keep.astype(F32) + hop(send, "core", 2, 1).astype(F32)).astype(BF)
    w_up_grad = jnp.sum(
        lax.all_to_all(both, ("ylo", "x"), 0, 0, tiled=True).astype(F32), axis=0
    )

    sums_abs = to_absolute(active_total.reshape(NZ, 2, hid_width)).astype(BF)
    all_sums = lax.all_to_all(
        jnp.broadcast_to(sums_abs[None], (16, 16, hid_width)), DP, 0, 0, tiled=True
    ).reshape(256, hid_width)
    slices = jnp.moveaxis(group_grad.reshape(16, 16, channels // 16), 1, 0)
    all_grads = lax.all_to_all(slices, DP, 0, 0, tiled=True).reshape(256, channels // 16)
    w_down_grad = jnp.dot(all_sums.T, all_grads, preferred_element_type=F32)

    img_grad = back_unit(image_sum, img_unit, img_len)
    txt_grad = back_unit(text_sum, txt_unit, txt_len)
    return (img_grad, txt_grad, w_up_grad, w_down_grad)


def solution(mesh):
    split = Mesh(mesh.devices.reshape(2, 4, 2, NZ, 2), ALL)
    in_specs = (
        P(ALL, None),
        P(ALL, None),
        P(ALL),
        P(ALL),
        P(),
        P(),
        P(ALL, None),
        P(),
        P(),
        P(),
        P(None, FSDP),
        P(FSDP, None),
        P(),
        P(),
        P(),
        P(),
    )
    out_specs = (P(ALL, None), P(ALL, None), P(DP, FSDP), P(FSDP, DP))
    return jax.shard_map(
        on_device, mesh=split, in_specs=in_specs, out_specs=out_specs, check_vma=False
    )
```

```python
import functools
import math

import jax
import jax.numpy as jnp
from jax import lax
from jax.experimental import pallas as pl
from jax.experimental.pallas import tpu as pltpu
from jax.sharding import Mesh
from jax.sharding import PartitionSpec as P

KERNEL = 7
SIDE = 8
PATCHES = SIDE * SIDE
DP = ("ylo", "x", "core")
FSDP = ("z", "yhi")
ALL = DP + FSDP
NZ = 8
PAIRS = 32
EMBED = 1024
WIDTH = 3072
HID = 384
SEG = WIDTH // EMBED
IMG_AT = SEG * PATCHES
ROWS = IMG_AT + PAIRS + 8
TXT_ROWS = PAIRS + 8
SLAB = WIDTH // 16
BF = jnp.bfloat16
F32 = jnp.float32

GROUPS = [[(0, 0), (0, 1)]]
for _step in range(1, NZ // 2):
    GROUPS.append([(NZ - _step, 0), (NZ - _step, 1), (_step, 0), (_step, 1)])
GROUPS.append([(NZ // 2, 0), (NZ // 2, 1)])
KEYS = [key for group in GROUPS for key in group]


def params(mib):
    return pltpu.CompilerParams(vmem_limit_bytes=mib << 20)


def whole(count):
    return [pl.BlockSpec(memory_space=pltpu.VMEM)] * count


def shape(rows, columns, dtype):
    return jax.ShapeDtypeStruct((rows, columns), dtype)


def hop(value, axis, length, step):
    return lax.ppermute(value, axis, [(i, (i + step) % length) for i in range(length)])


def absolute(key):
    z = lax.rem(lax.axis_index("z") + key[0], NZ)
    y = lax.axis_index("yhi")
    return z * 2 + (y if key[1] == 0 else 1 - y)


def unit_rows(values):
    length = jnp.sqrt(jnp.sum(values * values, axis=1, keepdims=True) + 1e-06)
    return (values / length, length)


def front_kernel(
    img, txt, img_ids, txt_ids, block_in, taps, gain, bias, blk, txt_pay, means, mixed, ids
):
    def id_rows(source):
        ids[...] = jnp.zeros_like(ids)
        ids[0:1, 0:PAIRS] = source[...]
        row = lax.broadcasted_iota(jnp.int32, (8, EMBED), 0)
        value = jnp.broadcast_to(ids[0:1, :], (8, EMBED))
        return jnp.where(row == 0, value >> 7, jnp.where(row == 1, value & 127, 0)).astype(F32)

    blk[IMG_AT : IMG_AT + PAIRS, :] = unit_rows(img[...].astype(F32))[0].astype(BF)
    blk[IMG_AT + PAIRS : ROWS, :] = id_rows(img_ids).astype(BF)
    txt_pay[0:PAIRS, :] = unit_rows(txt[...].astype(F32))[0].astype(BF)
    place = (lax.axis_index("ylo") * 4 + lax.axis_index("x")) * 2 + lax.axis_index("core")
    txt_pay[PAIRS:TXT_ROWS, :] = pltpu.roll(id_rows(txt_ids), place * PAIRS, 1).astype(BF)

    column = lax.broadcasted_iota(jnp.int32, (SIDE, 128), 0)

    def lanes(c, sums):
        at = pl.ds(pl.multiple_of(c * 128, 128), 128)
        patch = block_in[:, at].astype(F32)
        rows = [patch[r * SIDE : (r + 1) * SIDE] for r in range(SIDE)]
        total = rows[0]
        for r in range(1, SIDE):
            total = total + rows[r]
        mean = jnp.sum(total, axis=0, keepdims=True) / PATCHES
        means[0:1, at] = mean.astype(BF).astype(F32)
        acc = [jnp.zeros((SIDE, 128), F32) for _ in range(SIDE)]
        for across in range(KERNEL):
            move = across - KERNEL // 2
            if move == 0:
                moved = rows
            else:
                inside = (column + move >= 0) & (column + move < SIDE)
                moved = [
                    jnp.where(inside, pltpu.roll(row, (-move) % SIDE, 0), 0.0) for row in rows
                ]
            for above in range(KERNEL):
                tap = taps[above * KERNEL + across : above * KERNEL + across + 1, at]
                for r in range(SIDE):
                    source = r + above - KERNEL // 2
                    if 0 <= source < SIDE:
                        acc[r] = acc[r] + tap * moved[source]
        for r in range(SIDE):
            mixed[r * SIDE : (r + 1) * SIDE, at] = acc[r]
        return tuple(s + a for s, a in zip(sums, acc))

    sums = lax.fori_loop(
        0, WIDTH // 128, lanes, tuple(jnp.zeros((SIDE, 128), F32) for _ in range(SIDE))
    )
    centre = jnp.concatenate(
        [jnp.sum(s, axis=1, keepdims=True) / WIDTH for s in sums], axis=0
    )
    square = jnp.zeros((PATCHES, 128), F32)
    for c in range(WIDTH // 128):
        off = mixed[:, c * 128 : (c + 1) * 128] - centre
        square = square + off * off
    inverse = 1.0 / jnp.sqrt(jnp.sum(square, axis=1, keepdims=True) / WIDTH + 1e-06)
    for c in range(WIDTH // 128):
        at = slice(c * 128, (c + 1) * 128)
        normal = (mixed[:, at] - centre) * inverse
        seg, lane = divmod(c * 128, EMBED)
        blk[seg * PATCHES : (seg + 1) * PATCHES, lane : lane + 128] = (
            normal * gain[:, at] + bias[:, at]
        ).astype(BF)


def front(img, txt, img_ids, txt_ids, block_in, taps, gain, bias):
    return pl.pallas_call(
        front_kernel,
        out_shape=(shape(ROWS, EMBED, BF), shape(TXT_ROWS, EMBED, BF), shape(1, WIDTH, F32)),
        in_specs=whole(8),
        out_specs=tuple(whole(3)),
        scratch_shapes=[
            pltpu.VMEM((PATCHES, WIDTH), F32),
            pltpu.VMEM((8, EMBED), jnp.int32),
        ],
        compiler_params=params(16),
        name="front",
    )(img, txt, img_ids, txt_ids, block_in, taps, gain, bias)


def step_kernel(count, *refs):
    blocks = refs[:count]
    w_up, texts, temp_log, logit_bias, slope, sums, image_part, weights = refs[count:]
    root = math.sqrt(2.0 / math.pi)
    hidden = None
    for seg in range(SEG):
        rows = jnp.concatenate(
            [b[seg * PATCHES : (seg + 1) * PATCHES, :] for b in blocks], axis=0
        )
        part = jnp.dot(
            rows, w_up[seg * EMBED : (seg + 1) * EMBED, :], preferred_element_type=F32
        )
        hidden = part if hidden is None else hidden + part
    square = hidden * hidden
    curve = jnp.tanh(root * (hidden + 0.044715 * (square * hidden)))
    half = 0.5 * (1.0 + curve)
    active = (hidden * half).astype(BF).astype(F32)
    slope[...] = half + 0.5 * hidden * (1.0 - curve * curve) * (
        root * (1.0 + 3.0 * 0.044715 * square)
    )
    for i in range(count):
        sums[i : i + 1, :] = jnp.sum(
            active[i * PATCHES : (i + 1) * PATCHES], axis=0, keepdims=True
        )

    temper = jnp.exp(temp_log[...])
    text_rows = jnp.concatenate(
        [texts[d * TXT_ROWS : d * TXT_ROWS + PAIRS, :] for d in range(16)], axis=0
    )
    digits = texts[PAIRS : PAIRS + 8, 0:512].astype(F32)
    for d in range(1, 16):
        at = d * TXT_ROWS + PAIRS
        digits = digits + texts[at : at + 8, 0:512].astype(F32)
    text_ids = digits[0:1] * 128.0 + digits[1:2]
    columns = []
    for b in blocks:
        pair = b[IMG_AT + PAIRS : ROWS, 0:128].astype(F32)
        row = jnp.broadcast_to(pair[0:1] * 128.0 + pair[1:2], (128, 128))
        columns.append(jnp.transpose(row)[0:PAIRS, 0:1])
    image_ids = jnp.concatenate(columns, axis=0)
    images = jnp.concatenate([b[IMG_AT : IMG_AT + PAIRS, :] for b in blocks], axis=0)
    scores = lax.dot_general(
        images, text_rows, (((1,), (1,)), ((), ())), preferred_element_type=F32
    )
    logits = temper * scores + logit_bias[...]
    labels = jnp.where(image_ids == text_ids, 1.0, -1.0)
    weight = (temper * -labels * jax.nn.sigmoid(-labels * logits)).astype(BF)
    weights[...] = weight
    image_part[...] = jnp.dot(weight, text_rows, preferred_element_type=F32).astype(BF)


def step(blocks, w_up, texts, temp_log, logit_bias):
    count = len(blocks)
    return pl.pallas_call(
        functools.partial(step_kernel, count),
        out_shape=(
            shape(count * PATCHES, HID, F32),
            shape(count, HID, F32),
            shape(count * PAIRS, EMBED, BF),
            shape(count * PAIRS, 16 * PAIRS, BF),
        ),
        in_specs=whole(count + 4),
        out_specs=tuple(whole(4)),
        compiler_params=params(20),
        name="step",
    )(*blocks, w_up, texts, temp_log, logit_bias)


def mean_kernel(*refs):
    count = len(GROUPS)
    sums, images = refs[:count], refs[count : 2 * count]
    w_down, out, held = refs[2 * count :]
    mean = jnp.concatenate([s[...] for s in sums], axis=0) / PATCHES
    first = mean.astype(BF)
    rest = mean - first.astype(F32)
    second = rest.astype(BF)
    third = (rest - second.astype(F32)).astype(BF)
    three = jnp.dot(
        jnp.concatenate([first, second, third], axis=0), w_down[...], preferred_element_type=F32
    )
    partial = three[0:16] + three[16:32] + three[32:48]
    rows = jnp.concatenate(
        [
            image[i * PAIRS : i * PAIRS + 8, :].astype(F32)[0:1]
            for image, group in zip(images, GROUPS)
            for i in range(len(group))
        ],
        axis=0,
    )
    for c in range(6):
        held[:, c, :] = partial[:, c * 512 : (c + 1) * 512]
    for c in range(2):
        held[:, 6 + c, :] = rows[:, c * 512 : (c + 1) * 512]
    for j, key in enumerate(KEYS):
        at = pl.ds(pl.multiple_of(absolute(key) * 8, 8), 8)
        out[at, :] = held[j].astype(BF)


def mean_rows(sums, images, w_down):
    return pl.pallas_call(
        mean_kernel,
        out_shape=shape(128, 512, BF),
        in_specs=whole(2 * len(GROUPS) + 1),
        out_specs=pl.BlockSpec(memory_space=pltpu.VMEM),
        scratch_shapes=[pltpu.VMEM((16, 8, 512), F32)],
        compiler_params=params(16),
        name="mean_rows",
    )(*sums, *images, w_down)


def head_kernel(parts, means, scale, gain, bias, w_proj, out):
    total = parts[0:8, :].astype(F32)
    for d in range(1, 16):
        total = total + parts[d * 8 : (d + 1) * 8, :].astype(F32)
    block_mean = jnp.concatenate([total[c : c + 1] for c in range(6)], axis=1)
    image_sum = jnp.concatenate([total[6:7], total[7:8]], axis=1)
    pooled = means[...] + scale[...] * block_mean
    centred = pooled - jnp.sum(pooled, axis=1, keepdims=True) / WIDTH
    inverse = 1.0 / jnp.sqrt(jnp.sum(centred * centred, axis=1, keepdims=True) / WIDTH + 1e-06)
    head_norm = centred * inverse
    head_out = jnp.broadcast_to(head_norm * gain[...] + bias[...], (8, WIDTH)).astype(BF)
    embed = jnp.dot(head_out, w_proj[...], preferred_element_type=F32)[0:1]
    unit, length = unit_rows(embed)
    inner = jnp.sum(unit * image_sum, axis=1, keepdims=True)
    embed_grad = jnp.broadcast_to((image_sum - unit * inner) / length, (8, EMBED)).astype(BF)
    head_grad = lax.dot_general(
        embed_grad, w_proj[...], (((1,), (1,)), ((), ())), preferred_element_type=F32
    )[0:1]
    norm_grad = head_grad * gain[...]
    pool_grad = inverse * (
        norm_grad
        - jnp.sum(norm_grad, axis=1, keepdims=True) / WIDTH
        - head_norm * (jnp.sum(norm_grad * head_norm, axis=1, keepdims=True) / WIDTH)
    )
    row = scale[...] * pool_grad / PATCHES
    tile = jnp.concatenate([row[:, c * HID : (c + 1) * HID] for c in range(8)], axis=0).astype(BF)
    for d in range(16):
        out[d * 8 : (d + 1) * 8, :] = tile


def head(parts, means, scale, gain, bias, w_proj):
    return pl.pallas_call(
        head_kernel,
        out_shape=shape(128, HID, BF),
        in_specs=whole(6),
        out_specs=pl.BlockSpec(memory_space=pltpu.VMEM),
        compiler_params=params(16),
        name="head",
    )(parts, means, scale, gain, bias, w_proj)


def text_kernel(*refs):
    count = len(GROUPS)
    blocks = refs[:16]
    weights, images, sums = (refs[16 + i * count : 16 + (i + 1) * count] for i in range(3))
    txt_out, img_out = refs[16 + 3 * count :]
    weight = jnp.concatenate([w[...] for w in weights], axis=0)
    rows = jnp.concatenate([b[IMG_AT : IMG_AT + PAIRS, :] for b in blocks], axis=0)
    text_part = lax.dot_general(
        weight, rows, (((0,), (0,)), ((), ())), preferred_element_type=F32
    ).astype(BF)
    total = jnp.concatenate([s[...] for s in sums], axis=0)
    active = jnp.concatenate(
        [total[0:8], total[8:16], jnp.zeros((8, EMBED - 2 * HID), F32)], axis=1
    ).astype(BF)
    for d in range(16):
        txt_out[d * TXT_ROWS : d * TXT_ROWS + PAIRS, :] = text_part[d * PAIRS : (d + 1) * PAIRS]
        txt_out[d * TXT_ROWS + PAIRS : (d + 1) * TXT_ROWS, :] = active
    for image, group in zip(images, GROUPS):
        for i, key in enumerate(group):
            at = pl.ds(pl.multiple_of(absolute(key) * PAIRS, PAIRS), PAIRS)
            img_out[at, :] = image[i * PAIRS : (i + 1) * PAIRS, :]


def text_parts(blocks, weights, images, sums):
    return pl.pallas_call(
        text_kernel,
        out_shape=(shape(16 * TXT_ROWS, EMBED, BF), shape(16 * PAIRS, EMBED, BF)),
        in_specs=whole(16 + 3 * len(GROUPS)),
        out_specs=tuple(whole(2)),
        compiler_params=params(24),
        name="text_parts",
    )(*blocks, *weights, *images, *sums)


def turn_kernel(*refs):
    blocks, out = refs[:16], refs[16]
    for p in range(8):
        for seg in range(SEG):
            at = slice(seg * PATCHES, (seg + 1) * PATCHES)
            rows = jnp.concatenate([blocks[2 * p][at, :], blocks[2 * p + 1][at, :]], axis=0)
            out[seg * EMBED : (seg + 1) * EMBED, p * 128 : (p + 1) * 128] = jnp.transpose(rows)


def turned(blocks):
    return pl.pallas_call(
        turn_kernel,
        out_shape=shape(WIDTH, 16 * PATCHES, BF),
        in_specs=whole(16),
        out_specs=pl.BlockSpec(memory_space=pltpu.VMEM),
        compiler_params=params(24),
        name="turned",
    )(*blocks)


def back_kernel(*refs):
    count = len(GROUPS)
    grads, w_down, rows = refs[:3]
    slopes = refs[3 : 3 + count]
    send, keep, held, hid_grad = refs[3 + count :]
    for j, key in enumerate(KEYS):
        at = pl.ds(pl.multiple_of(absolute(key) * 8, 8), 8)
        held[j] = grads[at, :].astype(F32)
    group = jnp.concatenate([held[:, c, :] for c in range(8)], axis=1)
    row_down = lax.dot_general(
        group.astype(BF), w_down[...], (((1,), (1,)), ((), ())), preferred_element_type=F32
    )
    j = 0
    for slope, keys in zip(slopes, GROUPS):
        for i in range(len(keys)):
            hid_grad[j * PATCHES : (j + 1) * PATCHES, :] = (
                slope[i * PATCHES : (i + 1) * PATCHES, :] * row_down[j : j + 1]
            ).astype(BF)
            j += 1
    low, high = slice(0, SLAB), slice(SLAB, 2 * SLAB)
    core = lax.axis_index("core")
    for k in range(8):
        part = jnp.dot(
            rows[k * 2 * SLAB : (k + 1) * 2 * SLAB, :], hid_grad[...], preferred_element_type=F32
        ).astype(BF)
        mine = group[:, k * 2 * SLAB : (k + 1) * 2 * SLAB]
        swapped = pltpu.roll(mine, SLAB, 1).astype(BF)
        mine = mine.astype(BF)
        at = slice(k * (SLAB + 16), k * (SLAB + 16) + SLAB)
        below = slice(k * (SLAB + 16) + SLAB, (k + 1) * (SLAB + 16))

        @pl.when(core == 0)
        def _():
            keep[at, :] = part[low]
            send[at, :] = part[high]
            keep[below, :] = mine
            send[below, :] = swapped

        @pl.when(core == 1)
        def _():
            keep[at, :] = part[high]
            send[at, :] = part[low]
            keep[below, :] = swapped
            send[below, :] = mine


def backward(grads, w_down, rows, slopes):
    out = shape(8 * (SLAB + 16), HID, BF)
    return pl.pallas_call(
        back_kernel,
        out_shape=(out, out),
        in_specs=whole(3 + len(GROUPS)),
        out_specs=tuple(whole(2)),
        scratch_shapes=[pltpu.VMEM((16, 8, HID), F32), pltpu.VMEM((16 * PATCHES, HID), BF)],
        compiler_params=params(32),
        name="backward",
    )(grads, w_down, rows, *slopes)


def join_kernel(keep, got, out):
    lane = lax.broadcasted_iota(jnp.int32, (16, HID), 1)
    for k in range(8):
        at = slice(k * (SLAB + 16), k * (SLAB + 16) + SLAB)
        below = slice(k * (SLAB + 16) + SLAB, (k + 1) * (SLAB + 16))
        out[at, :] = (keep[at, :].astype(F32) + got[at, :].astype(F32)).astype(BF)
        other = pltpu.roll(got[below, :].astype(F32), SLAB, 1)
        out[below, :] = jnp.where(lane < SLAB, keep[below, :].astype(F32), other).astype(BF)


def join(keep, got):
    return pl.pallas_call(
        join_kernel,
        out_shape=shape(8 * (SLAB + 16), HID, BF),
        in_specs=whole(2),
        out_specs=pl.BlockSpec(memory_space=pltpu.VMEM),
        compiler_params=params(16),
        name="join",
    )(keep, got)


def last_kernel(got, texts, up_out, down_out):
    total = got[0:SLAB, :].astype(F32)
    for k in range(1, 8):
        at = k * (SLAB + 16)
        total = total + got[at : at + SLAB, :].astype(F32)
    up_out[...] = total
    core = lax.axis_index("core")
    grads = jnp.concatenate(
        [got[k * (SLAB + 16) + SLAB : (k + 1) * (SLAB + 16), :] for k in range(8)], axis=0
    )
    others = pltpu.roll(grads.astype(F32), SLAB, 1)[:, 0:SLAB].astype(BF)
    down = None
    for own, right in ((core, grads[:, 0:SLAB]), (1 - core, others)):
        pieces = []
        for k in range(8):
            at = pl.ds(pl.multiple_of((2 * k + own) * TXT_ROWS + PAIRS, 8), 8)
            pieces.append(texts[at, 0:HID])
            pieces.append(texts[at, HID : 2 * HID])
        left = jnp.concatenate(pieces, axis=0)
        part = lax.dot_general(
            left, right, (((0,), (0,)), ((), ())), preferred_element_type=F32
        )
        down = part if down is None else down + part
    down_out[...] = down


def last(got, texts):
    return pl.pallas_call(
        last_kernel,
        out_shape=(shape(SLAB, HID, F32), shape(HID, SLAB, F32)),
        in_specs=whole(2),
        out_specs=tuple(whole(2)),
        compiler_params=params(16),
        name="last",
    )(got, texts)


def rows_kernel(stride, parts, emb, out):
    total = parts[0:PAIRS, :].astype(F32)
    for d in range(1, 16):
        total = total + parts[d * stride : d * stride + PAIRS, :].astype(F32)
    unit, length = unit_rows(emb[...].astype(F32))
    inner = jnp.sum(unit * total, axis=1, keepdims=True)
    out[...] = (total - unit * inner) / length


def row_grads(parts, emb, stride, name):
    return pl.pallas_call(
        functools.partial(rows_kernel, stride),
        out_shape=shape(PAIRS, EMBED, F32),
        in_specs=whole(2),
        out_specs=pl.BlockSpec(memory_space=pltpu.VMEM),
        compiler_params=params(16),
        name=name,
    )(parts, emb)


def swap(value, axes, count):
    rows, columns = value.shape
    parts = value.reshape(count, rows // count, columns)
    return lax.all_to_all(parts, axes, 0, 0, tiled=True).reshape(rows, columns)


def on_device(
    img_emb,
    txt_emb,
    img_ids,
    txt_ids,
    temp_log,
    logit_bias,
    block_in,
    dw_kernel,
    ln_gain,
    ln_bias,
    w_up,
    w_down,
    layer_scale,
    head_gain,
    head_bias,
    w_proj,
):
    blk, txt_pay, means = front(
        img_emb,
        txt_emb,
        img_ids.reshape(1, PAIRS),
        txt_ids.reshape(1, PAIRS),
        block_in,
        dw_kernel,
        ln_gain.reshape(1, WIDTH),
        ln_bias.reshape(1, WIDTH),
    )
    got = {(0, 0): blk, (0, 1): hop(blk, "yhi", 2, 1)}
    for distance in range(1, NZ // 2 + 1):
        last_hop = distance == NZ // 2
        for side in range(2):
            if not last_hop or side == 0:
                got[NZ - distance, side] = hop(
                    got[(NZ - distance + 1) % NZ, side], "z", NZ, 1
                )
            if not last_hop or side == 1:
                got[distance, side] = hop(got[distance - 1, side], "z", NZ, -1)
    texts = swap(
        jnp.broadcast_to(txt_pay[None], (16, TXT_ROWS, EMBED)).reshape(-1, EMBED), DP, 16
    )
    temper = temp_log.reshape(1, 1)
    offset = logit_bias.reshape(1, 1)
    slopes, sums, images, weights = [], [], [], []
    for group in GROUPS:
        done = step([got[key] for key in group], w_up, texts, temper, offset)
        for into, value in zip((slopes, sums, images, weights), done):
            into.append(value)
    parts = swap(mean_rows(sums, images, w_down), FSDP, 16)
    blocks = [got[key] for key in KEYS]
    txt_parts, img_parts = text_parts(blocks, weights, images, sums)
    txt_parts = swap(txt_parts, DP, 16)
    rows = turned(blocks)
    grads = head(
        parts,
        means,
        layer_scale.reshape(1, WIDTH),
        head_gain.reshape(1, WIDTH),
        head_bias.reshape(1, WIDTH),
        w_proj,
    )
    grads = swap(grads, FSDP, 16)
    img_parts = swap(img_parts, FSDP, 16)
    send, keep = backward(grads, w_down, rows, slopes)
    both = join(keep, hop(send, "core", 2, 1))
    w_up_grad, w_down_grad = last(swap(both, ("ylo", "x"), 8), txt_parts)
    txt_grad = row_grads(txt_parts, txt_emb, TXT_ROWS, "txt_rows")
    img_grad = row_grads(img_parts, img_emb, PAIRS, "img_rows")
    return (img_grad, txt_grad, w_up_grad, w_down_grad)


def solution(mesh):
    split = Mesh(mesh.devices.reshape(2, 4, 2, NZ, 2), ALL)
    in_specs = (
        P(ALL, None),
        P(ALL, None),
        P(ALL),
        P(ALL),
        P(),
        P(),
        P(ALL, None),
        P(),
        P(),
        P(),
        P(None, FSDP),
        P(FSDP, None),
        P(),
        P(),
        P(),
        P(),
    )
    out_specs = (P(ALL, None), P(ALL, None), P(DP, FSDP), P(FSDP, DP))
    return jax.shard_map(
        on_device, mesh=split, in_specs=in_specs, out_specs=out_specs, check_vma=False
    )
```

```python
import functools
import math

import jax
import jax.numpy as jnp
from jax import lax
from jax.experimental import pallas as pl
from jax.experimental.pallas import tpu as pltpu
from jax.sharding import Mesh
from jax.sharding import PartitionSpec as P

KERNEL = 7
SIDE = 8
PATCHES = SIDE * SIDE
DP = ("ylo", "x", "core")
FSDP = ("z", "yhi")
ALL = DP + FSDP
NZ = 8
PAIRS = 32
EMBED = 1024
WIDTH = 3072
HID = 384
SEG = WIDTH // EMBED
IMG_AT = SEG * PATCHES
ROWS = IMG_AT + PAIRS + 8
TXT_ROWS = PAIRS + 8
SLAB = WIDTH // 16
HALF = SLAB + 16
FULL = HALF + 32
BF = jnp.bfloat16
F32 = jnp.float32

GROUPS = [[(0, 0), (0, 1)]]
for _step in range(1, NZ // 2):
    GROUPS.append([(NZ - _step, 0), (NZ - _step, 1), (_step, 0), (_step, 1)])
GROUPS.append([(NZ // 2, 0), (NZ // 2, 1)])
KEYS = [key for group in GROUPS for key in group]
UNITS = len(GROUPS)


def params(mib):
    return pltpu.CompilerParams(vmem_limit_bytes=mib << 20)


def cost(micros):
    return pl.CostEstimate(flops=0, transcendentals=0, bytes_accessed=int(micros * 3_690_000))


def whole(count):
    return [pl.BlockSpec(memory_space=pltpu.VMEM)] * count


def loose(count):
    return [pl.BlockSpec(memory_space=pl.ANY)] * count


def near(rows, columns, dtype):
    return jax.ShapeDtypeStruct((rows, columns), dtype)


def far(rows, columns, dtype):
    return pltpu.HBM((rows, columns), dtype)


def from_far(*arrays):
    return [pltpu.with_memory_space_constraint(array, pltpu.HBM) for array in arrays]


def hop(value, axis, length, step):
    return lax.ppermute(value, axis, [(i, (i + step) % length) for i in range(length)])


def absolute(key):
    z = lax.rem(lax.axis_index("z") + key[0], NZ)
    y = lax.axis_index("yhi")
    return z * 2 + (y if key[1] == 0 else 1 - y)


def unit_rows(values):
    length = jnp.sqrt(jnp.sum(values * values, axis=1, keepdims=True) + 1e-06)
    return (values / length, length)


def front_kernel(
    img, txt, img_ids, txt_ids, block_in, taps, gain, bias, blk, txt_all, means, mixed, ids, txt_pay, sems
):
    def id_rows(source):
        ids[...] = jnp.zeros_like(ids)
        ids[0:1, 0:PAIRS] = source[...]
        row = lax.broadcasted_iota(jnp.int32, (8, EMBED), 0)
        value = jnp.broadcast_to(ids[0:1, :], (8, EMBED))
        return jnp.where(row == 0, value >> 7, jnp.where(row == 1, value & 127, 0)).astype(F32)

    blk[IMG_AT : IMG_AT + PAIRS, :] = unit_rows(img[...].astype(F32))[0].astype(BF)
    blk[IMG_AT + PAIRS : ROWS, :] = id_rows(img_ids).astype(BF)
    txt_pay[0:PAIRS, :] = unit_rows(txt[...].astype(F32))[0].astype(BF)
    place = (lax.axis_index("ylo") * 4 + lax.axis_index("x")) * 2 + lax.axis_index("core")
    txt_pay[PAIRS:TXT_ROWS, :] = pltpu.roll(id_rows(txt_ids), place * PAIRS, 1).astype(BF)

    copies = [
        pltpu.make_async_copy(
            txt_pay, txt_all.at[d * TXT_ROWS : (d + 1) * TXT_ROWS, :], sems.at[d]
        )
        for d in range(16)
    ]
    for copy in copies:
        copy.start()

    column = lax.broadcasted_iota(jnp.int32, (SIDE, 128), 0)

    def lanes(c, sums):
        at = pl.ds(pl.multiple_of(c * 128, 128), 128)
        patch = block_in[:, at].astype(F32)
        rows = [patch[r * SIDE : (r + 1) * SIDE] for r in range(SIDE)]
        total = rows[0]
        for r in range(1, SIDE):
            total = total + rows[r]
        mean = jnp.sum(total, axis=0, keepdims=True) / PATCHES
        means[0:1, at] = mean.astype(BF).astype(F32)
        acc = [jnp.zeros((SIDE, 128), F32) for _ in range(SIDE)]
        for across in range(KERNEL):
            move = across - KERNEL // 2
            if move == 0:
                moved = rows
            else:
                inside = (column + move >= 0) & (column + move < SIDE)
                moved = [
                    jnp.where(inside, pltpu.roll(row, (-move) % SIDE, 0), 0.0) for row in rows
                ]
            for above in range(KERNEL):
                tap = taps[above * KERNEL + across : above * KERNEL + across + 1, at]
                for r in range(SIDE):
                    source = r + above - KERNEL // 2
                    if 0 <= source < SIDE:
                        acc[r] = acc[r] + tap * moved[source]
        for r in range(SIDE):
            mixed[r * SIDE : (r + 1) * SIDE, at] = acc[r]
        return tuple(s + a for s, a in zip(sums, acc))

    sums = lax.fori_loop(
        0, WIDTH // 128, lanes, tuple(jnp.zeros((SIDE, 128), F32) for _ in range(SIDE))
    )
    centre = jnp.concatenate(
        [jnp.sum(s, axis=1, keepdims=True) / WIDTH for s in sums], axis=0
    )
    square = jnp.zeros((PATCHES, 128), F32)
    for c in range(WIDTH // 128):
        off = mixed[:, c * 128 : (c + 1) * 128] - centre
        square = square + off * off
    inverse = 1.0 / jnp.sqrt(jnp.sum(square, axis=1, keepdims=True) / WIDTH + 1e-06)
    for c in range(WIDTH // 128):
        at = slice(c * 128, (c + 1) * 128)
        normal = (mixed[:, at] - centre) * inverse
        seg, lane = divmod(c * 128, EMBED)
        blk[seg * PATCHES : (seg + 1) * PATCHES, lane : lane + 128] = (
            normal * gain[:, at] + bias[:, at]
        ).astype(BF)
    for copy in copies:
        copy.wait()


def front(*args):
    return pl.pallas_call(
        front_kernel,
        out_shape=(
            near(ROWS, EMBED, BF),
            far(16 * TXT_ROWS, EMBED, BF),
            far(1, WIDTH, F32),
        ),
        out_specs=(pl.BlockSpec(), *loose(1), pl.BlockSpec()),
        scratch_shapes=[
            pltpu.VMEM((PATCHES, WIDTH), F32),
            pltpu.VMEM((8, EMBED), jnp.int32),
            pltpu.VMEM((TXT_ROWS, EMBED), BF),
            pltpu.SemaphoreType.DMA((16,)),
        ],
        compiler_params=params(8),
        cost_estimate=cost(4.5),
        name="front",
    )(*from_far(*args))


def turn_into(blocks, turn):
    for seg in range(SEG):
        at = slice(seg * PATCHES, (seg + 1) * PATCHES)
        for p in range(len(blocks) // 2):
            rows = jnp.concatenate([b[at, :] for b in blocks[2 * p : 2 * p + 2]], axis=0)
            turn[seg * EMBED : (seg + 1) * EMBED, p * 128 : (p + 1) * 128] = jnp.transpose(rows)


def step_kernel(count, *refs):
    blocks, refs = refs[:count], refs[count:]
    w_up, texts, temp_log, logit_bias, *refs = refs
    outs, (sums, firsts), scratch, sems = refs[:4], refs[4:6], refs[6:10], refs[10]
    slope, image_part, weights, turn = scratch
    copies = [
        pltpu.make_async_copy(source, into, sems.at[i])
        for i, (source, into) in enumerate(zip(scratch, outs))
    ]
    turn_into(blocks, turn)
    copies[3].start()
    root = math.sqrt(2.0 / math.pi)
    hidden = None
    for seg in range(SEG):
        rows = jnp.concatenate(
            [b[seg * PATCHES : (seg + 1) * PATCHES, :] for b in blocks], axis=0
        )
        part = jnp.dot(
            rows, w_up[seg * EMBED : (seg + 1) * EMBED, :], preferred_element_type=F32
        )
        hidden = part if hidden is None else hidden + part
    square = hidden * hidden
    curve = jnp.tanh(root * (hidden + 0.044715 * (square * hidden)))
    half = 0.5 * (1.0 + curve)
    active = (hidden * half).astype(BF).astype(F32)
    slope[...] = half + 0.5 * hidden * (1.0 - curve * curve) * (
        root * (1.0 + 3.0 * 0.044715 * square)
    )
    copies[0].start()
    for i in range(count):
        sums[i : i + 1, :] = jnp.sum(
            active[i * PATCHES : (i + 1) * PATCHES], axis=0, keepdims=True
        )

    temper = jnp.exp(temp_log[...])
    text_rows = jnp.concatenate(
        [texts[d * TXT_ROWS : d * TXT_ROWS + PAIRS, :] for d in range(16)], axis=0
    )
    digits = texts[PAIRS : PAIRS + 8, 0:512].astype(F32)
    for d in range(1, 16):
        at = d * TXT_ROWS + PAIRS
        digits = digits + texts[at : at + 8, 0:512].astype(F32)
    text_ids = digits[0:1] * 128.0 + digits[1:2]
    columns = []
    for b in blocks:
        pair = b[IMG_AT + PAIRS : ROWS, 0:128].astype(F32)
        row = jnp.broadcast_to(pair[0:1] * 128.0 + pair[1:2], (128, 128))
        columns.append(jnp.transpose(row)[0:PAIRS, 0:1])
    image_ids = jnp.concatenate(columns, axis=0)
    images = jnp.concatenate([b[IMG_AT : IMG_AT + PAIRS, :] for b in blocks], axis=0)
    scores = lax.dot_general(
        images, text_rows, (((1,), (1,)), ((), ())), preferred_element_type=F32
    )
    logits = temper * scores + logit_bias[...]
    labels = jnp.where(image_ids == text_ids, 1.0, -1.0)
    weight = (temper * -labels * jax.nn.sigmoid(-labels * logits)).astype(BF)
    weights[...] = weight
    copies[2].start()
    image = jnp.dot(weight, text_rows, preferred_element_type=F32)
    image_part[...] = image.astype(BF)
    copies[1].start()
    for i in range(count):
        firsts[i : i + 1, :] = image[i * PAIRS : i * PAIRS + 1]
    for copy in copies:
        copy.wait()


def step(blocks, w_up, texts, temp_log, logit_bias):
    count = len(blocks)
    dims = [
        (count * PATCHES, HID, F32),
        (count * PAIRS, EMBED, BF),
        (count * PAIRS, 16 * PAIRS, BF),
        (WIDTH, count * PATCHES, BF),
    ]
    return pl.pallas_call(
        functools.partial(step_kernel, count),
        out_shape=(
            *(far(*dim) for dim in dims),
            near(count, HID, F32),
            near(count, EMBED, F32),
        ),
        in_specs=whole(count + 4),
        out_specs=(*loose(4), *whole(2)),
        scratch_shapes=[pltpu.VMEM(dim[:2], dim[2]) for dim in dims]
        + [pltpu.SemaphoreType.DMA((4,))],
        compiler_params=params(14),
        cost_estimate=cost(1.5 + 0.8 * count),
        name="step",
    )(*blocks, w_up, texts, temp_log, logit_bias)


def mean_kernel(*refs):
    count = UNITS
    sums, firsts = refs[:count], refs[count : 2 * count]
    w_down, out, held = refs[2 * count :]
    mean = jnp.concatenate([s[...] for s in sums], axis=0) / PATCHES
    first = mean.astype(BF)
    rest = mean - first.astype(F32)
    second = rest.astype(BF)
    third = (rest - second.astype(F32)).astype(BF)
    three = jnp.dot(
        jnp.concatenate([first, second, third], axis=0), w_down[...], preferred_element_type=F32
    )
    partial = three[0:16] + three[16:32] + three[32:48]
    rows = jnp.concatenate([f[...] for f in firsts], axis=0)
    for c in range(6):
        held[:, c, :] = partial[:, c * 512 : (c + 1) * 512]
    for c in range(2):
        held[:, 6 + c, :] = rows[:, c * 512 : (c + 1) * 512]
    for j, key in enumerate(KEYS):
        at = pl.ds(pl.multiple_of(absolute(key) * 8, 8), 8)
        out[at, :] = held[j].astype(BF)


def mean_rows(sums, firsts, w_down):
    return pl.pallas_call(
        mean_kernel,
        out_shape=far(128, 512, BF),
        in_specs=whole(2 * len(GROUPS) + 1),
        scratch_shapes=[pltpu.VMEM((16, 8, 512), F32)],
        compiler_params=params(6),
        cost_estimate=cost(0.8),
        name="mean_rows",
    )(*sums, *firsts, w_down)


def head_kernel(parts, means, scale, gain, bias, w_far, out, w_proj, sems):
    quarter = WIDTH // 4
    copies = [
        pltpu.make_async_copy(
            w_far.at[i * quarter : (i + 1) * quarter, :],
            w_proj.at[i * quarter : (i + 1) * quarter, :],
            sems.at[i],
        )
        for i in range(4)
    ]
    for copy in copies:
        copy.start()
    total = parts[0:8, :].astype(F32)
    for d in range(1, 16):
        total = total + parts[d * 8 : (d + 1) * 8, :].astype(F32)
    block_mean = jnp.concatenate([total[c : c + 1] for c in range(6)], axis=1)
    image_sum = jnp.concatenate([total[6:7], total[7:8]], axis=1)
    pooled = means[...] + scale[...] * block_mean
    centred = pooled - jnp.sum(pooled, axis=1, keepdims=True) / WIDTH
    inverse = 1.0 / jnp.sqrt(jnp.sum(centred * centred, axis=1, keepdims=True) / WIDTH + 1e-06)
    head_norm = centred * inverse
    head_out = jnp.broadcast_to(head_norm * gain[...] + bias[...], (8, WIDTH)).astype(BF)
    embed = None
    for i in range(4):
        at = slice(i * quarter, (i + 1) * quarter)
        copies[i].wait()
        piece = jnp.dot(head_out[:, at], w_proj[at, :], preferred_element_type=F32)
        embed = piece if embed is None else embed + piece
    embed = embed[0:1]
    unit, length = unit_rows(embed)
    inner = jnp.sum(unit * image_sum, axis=1, keepdims=True)
    embed_grad = jnp.broadcast_to((image_sum - unit * inner) / length, (8, EMBED)).astype(BF)
    head_grad = lax.dot_general(
        embed_grad, w_proj[...], (((1,), (1,)), ((), ())), preferred_element_type=F32
    )[0:1]
    norm_grad = head_grad * gain[...]
    pool_grad = inverse * (
        norm_grad
        - jnp.sum(norm_grad, axis=1, keepdims=True) / WIDTH
        - head_norm * (jnp.sum(norm_grad * head_norm, axis=1, keepdims=True) / WIDTH)
    )
    row = scale[...] * pool_grad / PATCHES
    tile = jnp.concatenate([row[:, c * HID : (c + 1) * HID] for c in range(8)], axis=0).astype(BF)
    for d in range(16):
        out[d * 8 : (d + 1) * 8, :] = tile


def head(parts, means, scale, gain, bias, w_proj):
    return pl.pallas_call(
        head_kernel,
        out_shape=far(128, HID, BF),
        in_specs=whole(5) + loose(1),
        scratch_shapes=[pltpu.VMEM((WIDTH, EMBED), BF), pltpu.SemaphoreType.DMA((4,))],
        compiler_params=params(14),
        cost_estimate=cost(5.0),
        name="head",
    )(parts, *from_far(means, scale, gain, bias, w_proj))


def text_kernel(*refs):
    blocks = refs[:16]
    weights, images = (refs[16 + i * UNITS : 16 + (i + 1) * UNITS] for i in range(2))
    txt_send, txt_keep, img_send, img_keep, rows, weight, image, sems = refs[16 + 2 * UNITS :]
    copies, first = [], 0
    for u, group in enumerate(GROUPS):
        at = slice(first, first + len(group) * PAIRS)
        first += len(group) * PAIRS
        copies.append(pltpu.make_async_copy(weights[u], weight.at[at, :], sems.at[2 * u]))
        copies.append(pltpu.make_async_copy(images[u], image.at[at, :], sems.at[2 * u + 1]))
    for i in range(16):
        at = slice(i * PAIRS, (i + 1) * PAIRS)
        source = blocks[i].at[IMG_AT : IMG_AT + PAIRS, :]
        copies.append(pltpu.make_async_copy(source, rows.at[at, :], sems.at[2 * UNITS + i]))
    for copy in copies:
        copy.start()
    for copy in copies:
        copy.wait()
    text_part = lax.dot_general(
        weight[...], rows[...], (((0,), (0,)), ((), ())), preferred_element_type=F32
    ).astype(BF)
    core = lax.axis_index("core")
    for k in range(8):
        at = slice(k * PAIRS, (k + 1) * PAIRS)
        even = text_part[2 * k * PAIRS : (2 * k + 1) * PAIRS]
        odd = text_part[(2 * k + 1) * PAIRS : (2 * k + 2) * PAIRS]

        @pl.when(core == 0)
        def _():
            txt_keep[at, :] = even
            txt_send[at, :] = odd

        @pl.when(core == 1)
        def _():
            txt_keep[at, :] = odd
            txt_send[at, :] = even

    z = lax.axis_index("z")
    for j, (offset, side) in enumerate(KEYS):
        owner = lax.rem(z + offset, NZ)
        place = (owner & 1) * 4 + (owner & 2) + (owner >> 2)
        at = pl.ds(pl.multiple_of(place * PAIRS, PAIRS), PAIRS)
        into = img_keep if side == 0 else img_send
        into[at, :] = image[j * PAIRS : (j + 1) * PAIRS, :]


def text_parts(blocks, weights, images):
    return pl.pallas_call(
        text_kernel,
        out_shape=(far(8 * PAIRS, EMBED, BF),) * 4,
        in_specs=loose(16 + 2 * UNITS),
        out_specs=tuple(whole(4)),
        scratch_shapes=[
            pltpu.VMEM((16 * PAIRS, EMBED), BF),
            pltpu.VMEM((16 * PAIRS, 16 * PAIRS), BF),
            pltpu.VMEM((16 * PAIRS, EMBED), BF),
            pltpu.SemaphoreType.DMA((16 + 2 * UNITS,)),
        ],
        compiler_params=params(14),
        cost_estimate=cost(3.8),
        name="text_parts",
    )(*blocks, *from_far(*weights, *images))


def halve_kernel(bits, *refs):
    keeps, gots, sends, outs = (refs[2 * i : 2 * i + 2] for i in range(4))
    for (axis, shift), first, second, send, keep in zip(bits, keeps, gots, sends, outs):
        mine = (lax.axis_index(axis) >> shift) & 1
        rows = send.shape[0]
        for part in range(2):
            at = slice(part * rows, (part + 1) * rows)
            total = (first[at, :].astype(F32) + second[at, :].astype(F32)).astype(BF)

            @pl.when(mine == part)
            def _():
                keep[...] = total

            @pl.when(mine != part)
            def _():
                send[...] = total


def halved(bits, keeps, gots):
    outs = pl.pallas_call(
        functools.partial(halve_kernel, bits),
        out_shape=(far(keeps[0].shape[0] // 2, EMBED, BF),) * 4,
        in_specs=whole(4),
        compiler_params=params(8),
        cost_estimate=cost(1.5),
        name="halved",
    )(*from_far(*keeps), *gots)
    return outs[:2], outs[2:]


def partner(value, axis, length, bit):
    return lax.ppermute(value, axis, [(i, i ^ bit) for i in range(length)])


def back_kernel(*refs):
    grads, w_down = refs[:2]
    sums, slopes, turns = (refs[2 + i * UNITS : 2 + (i + 1) * UNITS] for i in range(3))
    send, keep, held, hid_grad, slope, rows, sems = refs[2 + 3 * UNITS :]
    slope_copies, low_copies, high_copies, first = [], [], [], 0
    low, high = slice(0, WIDTH // 2), slice(WIDTH // 2, WIDTH)
    for u, group in enumerate(GROUPS):
        at = slice(first, first + len(group) * PATCHES)
        first += len(group) * PATCHES
        slope_copies.append(pltpu.make_async_copy(slopes[u], slope.at[at, :], sems.at[3 * u]))
        for half, into, sem in ((low, low_copies, 1), (high, high_copies, 2)):
            into.append(
                pltpu.make_async_copy(
                    turns[u].at[half, :], rows.at[half, at], sems.at[3 * u + sem]
                )
            )
    for copy in (*slope_copies, *low_copies, *high_copies):
        copy.start()
    total = jnp.concatenate([s[...] for s in sums], axis=0).astype(BF)
    keep[8 * HALF :, :] = total
    send[8 * HALF :, :] = total
    for j, key in enumerate(KEYS):
        at = pl.ds(pl.multiple_of(absolute(key) * 8, 8), 8)
        held[j] = grads[at, :].astype(F32)
    group = jnp.concatenate([held[:, c, :] for c in range(8)], axis=1)
    row_down = lax.dot_general(
        group.astype(BF), w_down[...], (((1,), (1,)), ((), ())), preferred_element_type=F32
    )
    for copy in slope_copies:
        copy.wait()
    for j in range(16):
        at = slice(j * PATCHES, (j + 1) * PATCHES)
        hid_grad[at, :] = (slope[at, :] * row_down[j : j + 1]).astype(BF)
    for copy in low_copies:
        copy.wait()
    low, high = slice(0, SLAB), slice(SLAB, 2 * SLAB)
    core = lax.axis_index("core")
    for k in range(8):
        if k == 4:
            for copy in high_copies:
                copy.wait()
        part = jnp.dot(
            rows[k * 2 * SLAB : (k + 1) * 2 * SLAB, :], hid_grad[...], preferred_element_type=F32
        ).astype(BF)
        mine = group[:, k * 2 * SLAB : (k + 1) * 2 * SLAB]
        swapped = pltpu.roll(mine, SLAB, 1).astype(BF)
        mine = mine.astype(BF)
        at = slice(k * HALF, k * HALF + SLAB)
        below = slice(k * HALF + SLAB, (k + 1) * HALF)

        @pl.when(core == 0)
        def _():
            keep[at, :] = part[low]
            send[at, :] = part[high]
            keep[below, :] = mine
            send[below, :] = swapped

        @pl.when(core == 1)
        def _():
            keep[at, :] = part[high]
            send[at, :] = part[low]
            keep[below, :] = swapped
            send[below, :] = mine


def backward(grads, w_down, sums, slopes, turns):
    return pl.pallas_call(
        back_kernel,
        out_shape=(near(8 * HALF + 16, HID, BF),) * 2,
        in_specs=whole(2 + UNITS) + loose(2 * UNITS),
        out_specs=tuple(whole(2)),
        scratch_shapes=[
            pltpu.VMEM((16, 8, HID), F32),
            pltpu.VMEM((16 * PATCHES, HID), BF),
            pltpu.VMEM((16 * PATCHES, HID), F32),
            pltpu.VMEM((WIDTH, 16 * PATCHES), BF),
            pltpu.SemaphoreType.DMA((3 * UNITS,)),
        ],
        compiler_params=params(16),
        cost_estimate=cost(6.5),
        name="backward",
    )(grads, w_down, *sums, *from_far(*slopes, *turns))


def join_kernel(keep, got, out):
    lane = lax.broadcasted_iota(jnp.int32, (16, HID), 1)
    for k in range(8):
        at = slice(k * HALF, k * HALF + SLAB)
        below = slice(k * HALF + SLAB, (k + 1) * HALF)
        to = k * FULL
        out[to : to + SLAB, :] = (keep[at, :].astype(F32) + got[at, :].astype(F32)).astype(BF)
        other = pltpu.roll(got[below, :].astype(F32), SLAB, 1)
        out[to + SLAB : to + HALF, :] = jnp.where(
            lane < SLAB, keep[below, :].astype(F32), other
        ).astype(BF)
        out[to + HALF : to + HALF + 16, :] = keep[8 * HALF :, :]
        out[to + HALF + 16 : to + FULL, :] = got[8 * HALF :, :]


def join(keep, got):
    return pl.pallas_call(
        join_kernel,
        out_shape=far(8 * FULL, HID, BF),
        in_specs=whole(2),
        compiler_params=params(12),
        cost_estimate=cost(1.0),
        name="join",
    )(keep, got)


def last_kernel(got, up_out, down_out):
    total = got[0:SLAB, :].astype(F32)
    for k in range(1, 8):
        total = total + got[k * FULL : k * FULL + SLAB, :].astype(F32)
    up_out[...] = total
    grads = jnp.concatenate(
        [got[k * FULL + SLAB : k * FULL + HALF, :] for k in range(8)], axis=0
    )
    others = pltpu.roll(grads.astype(F32), SLAB, 1).astype(BF)
    down = None
    for side, left in enumerate((grads, others)):
        right = jnp.concatenate(
            [
                got[k * FULL + HALF + side * 16 : k * FULL + HALF + side * 16 + 16, :]
                for k in range(8)
            ],
            axis=0,
        )
        part = lax.dot_general(
            left, right, (((0,), (0,)), ((), ())), preferred_element_type=F32
        )
        down = part if down is None else down + part
    down_out[...] = down[0:SLAB, :]


def last(got):
    return pl.pallas_call(
        last_kernel,
        out_shape=(far(SLAB, HID, F32), far(SLAB, HID, F32)),
        in_specs=whole(1),
        compiler_params=params(12),
        cost_estimate=cost(2.0),
        name="last",
    )(got)


def rows_kernel(count, *refs):
    emb, out = refs[count:]
    total = None
    for ref in refs[:count]:
        for d in range(ref.shape[0] // PAIRS):
            part = ref[d * PAIRS : (d + 1) * PAIRS, :].astype(F32)
            total = part if total is None else total + part
    unit, length = unit_rows(emb[...].astype(F32))
    inner = jnp.sum(unit * total, axis=1, keepdims=True)
    out[...] = (total - unit * inner) / length


def row_grads(parts, emb, name):
    return pl.pallas_call(
        functools.partial(rows_kernel, len(parts)),
        out_shape=far(PAIRS, EMBED, F32),
        compiler_params=params(8),
        cost_estimate=cost(0.9),
        name=name,
    )(*parts, *from_far(emb))


def swap(value, axes, count):
    rows, columns = value.shape
    parts = value.reshape(count, rows // count, columns)
    return lax.all_to_all(parts, axes, 0, 0, tiled=True).reshape(rows, columns)


def on_device(
    img_emb,
    txt_emb,
    img_ids,
    txt_ids,
    temp_log,
    logit_bias,
    block_in,
    dw_kernel,
    ln_gain,
    ln_bias,
    w_up,
    w_down,
    layer_scale,
    head_gain,
    head_bias,
    w_proj,
):
    blk, txt_all, means = front(
        img_emb,
        txt_emb,
        img_ids.reshape(1, PAIRS),
        txt_ids.reshape(1, PAIRS),
        block_in,
        dw_kernel,
        ln_gain.reshape(1, WIDTH),
        ln_bias.reshape(1, WIDTH),
    )
    temper = temp_log.reshape(1, 1)
    offset = logit_bias.reshape(1, 1)
    got = {(0, 0): blk}
    kept = []

    def send_on(side, distance, up=True, down=True):
        if up:
            got[NZ - distance, side] = hop(got[(NZ - distance + 1) % NZ, side], "z", NZ, 1)
        if down:
            got[distance, side] = hop(got[distance - 1, side], "z", NZ, -1)

    def tie(keys, *values):
        tied = lax.optimization_barrier((*(got[key] for key in keys), *values))
        got.update(zip(keys, tied))
        return tied[len(keys) :]

    def work(unit):
        return step([got[key] for key in GROUPS[unit]], w_up, texts, temper, offset)

    got[0, 1] = hop(blk, "yhi", 2, 1)
    texts = swap(txt_all, DP, 16)
    for distance in range(1, NZ // 2):
        send_on(0, distance)
        send_on(1, distance)
    send_on(0, NZ // 2, down=False)
    done = tie([(3, 1)], *work(0), *work(1))
    send_on(1, NZ // 2, up=False)
    kept += [done[:6], done[6:]]
    kept += [work(unit) for unit in range(2, UNITS)]

    slopes, images, weights, turns, sums, firsts = zip(*kept)
    means_out, *weights = lax.optimization_barrier((mean_rows(sums, firsts, w_down), *weights))
    parts = swap(means_out, FSDP, 16)
    txt_send, txt_keep, img_send, img_keep = text_parts(
        [got[key] for key in KEYS], weights, images
    )
    keeps = (txt_keep, img_keep)
    gots = (hop(txt_send, "core", 2, 1), hop(img_send, "yhi", 2, 1))
    parts, txt_got = lax.optimization_barrier((parts, gots[0]))
    grads = head(
        parts,
        means,
        layer_scale.reshape(1, WIDTH),
        head_gain.reshape(1, WIDTH),
        head_bias.reshape(1, WIDTH),
        w_proj,
    )
    grads, img_got = lax.optimization_barrier((grads, gots[1]))
    grads = swap(grads, FSDP, 16)
    sends, keeps = halved((("ylo", 0), ("z", 0)), keeps, (txt_got, img_got))
    gots = (partner(sends[0], "ylo", 2, 1), partner(sends[1], "z", NZ, 1))
    grads, *gots = lax.optimization_barrier((grads, *gots))
    send, keep = backward(grads, w_down, sums, slopes, turns)
    sends, keeps = halved((("x", 1), ("z", 1)), keeps, gots)
    send, *sends = lax.optimization_barrier((send, *sends))
    gots = (partner(sends[0], "x", 4, 2), partner(sends[1], "z", NZ, 2))
    got_core, *gots = lax.optimization_barrier((hop(send, "core", 2, 1), *gots))
    both = join(keep, got_core)
    sends, keeps = halved((("x", 0), ("z", 2)), keeps, gots)
    w_up_grad, w_down_grad = last(swap(both, ("ylo", "x"), 8))
    w_down_grad = w_down_grad.T
    txt_grad = row_grads((keeps[0], partner(sends[0], "x", 4, 1)), txt_emb, "txt_rows")
    img_grad = row_grads((keeps[1], partner(sends[1], "z", NZ, 4)), img_emb, "img_rows")
    return (img_grad, txt_grad, w_up_grad, w_down_grad)


def solution(mesh):
    split = Mesh(mesh.devices.reshape(2, 4, 2, NZ, 2), ALL)
    in_specs = (
        P(ALL, None),
        P(ALL, None),
        P(ALL),
        P(ALL),
        P(),
        P(),
        P(ALL, None),
        P(),
        P(),
        P(),
        P(None, FSDP),
        P(FSDP, None),
        P(),
        P(),
        P(),
        P(),
    )
    out_specs = (P(ALL, None), P(ALL, None), P(DP, FSDP), P(FSDP, DP))
    return jax.shard_map(
        on_device, mesh=split, in_specs=in_specs, out_specs=out_specs, check_vma=False
    )
```

```python
import functools
import math

import jax
import jax.numpy as jnp
from jax import lax
from jax.experimental import pallas as pl
from jax.experimental.pallas import tpu as pltpu
from jax.sharding import Mesh
from jax.sharding import PartitionSpec as P

KERNEL = 7
SIDE = 8
PATCHES = SIDE * SIDE
DP = ("ylo", "x", "core")
FSDP = ("z", "yhi")
ALL = DP + FSDP
NZ = 8
PAIRS = 32
EMBED = 1024
WIDTH = 3072
HID = 384
SEG = WIDTH // EMBED
IMG_AT = SEG * PATCHES
ROWS = IMG_AT + PAIRS + 8
TXT_ROWS = PAIRS + 8
SLAB = WIDTH // 16
HALF = SLAB + 16
FULL = HALF + 32
BF = jnp.bfloat16
F32 = jnp.float32

GROUPS = [[(0, 0), (0, 1)]]
for _step in range(1, NZ // 2):
    GROUPS.append([(NZ - _step, 0), (NZ - _step, 1), (_step, 0), (_step, 1)])
GROUPS.append([(NZ // 2, 0), (NZ // 2, 1)])
KEYS = [key for group in GROUPS for key in group]
UNITS = len(GROUPS)


def params(mib):
    return pltpu.CompilerParams(vmem_limit_bytes=mib << 20)


def cost(micros):
    return pl.CostEstimate(flops=0, transcendentals=0, bytes_accessed=int(micros * 3_690_000))


def whole(count):
    return [pl.BlockSpec(memory_space=pltpu.VMEM)] * count


def loose(count):
    return [pl.BlockSpec(memory_space=pl.ANY)] * count


def near(rows, columns, dtype):
    return jax.ShapeDtypeStruct((rows, columns), dtype)


def far(rows, columns, dtype):
    return pltpu.HBM((rows, columns), dtype)


def from_far(*arrays):
    return [pltpu.with_memory_space_constraint(array, pltpu.HBM) for array in arrays]


def hop(value, axis, length, step):
    return lax.ppermute(value, axis, [(i, (i + step) % length) for i in range(length)])


def absolute(key):
    z = lax.rem(lax.axis_index("z") + key[0], NZ)
    y = lax.axis_index("yhi")
    return z * 2 + (y if key[1] == 0 else 1 - y)


def unit_rows(values):
    length = jnp.sqrt(jnp.sum(values * values, axis=1, keepdims=True) + 1e-06)
    return (values / length, length)


def id_rows(source, ids):
    ids[...] = jnp.zeros_like(ids)
    ids[0:1, 0:PAIRS] = source[...]
    row = lax.broadcasted_iota(jnp.int32, (8, EMBED), 0)
    value = jnp.broadcast_to(ids[0:1, :], (8, EMBED))
    return jnp.where(row == 0, value >> 7, jnp.where(row == 1, value & 127, 0)).astype(F32)


def text_rows_kernel(txt, txt_ids, txt_all, ids, txt_pay, sems):
    txt_pay[0:PAIRS, :] = unit_rows(txt[...].astype(F32))[0].astype(BF)
    place = (lax.axis_index("ylo") * 4 + lax.axis_index("x")) * 2 + lax.axis_index("core")
    txt_pay[PAIRS:TXT_ROWS, :] = pltpu.roll(id_rows(txt_ids, ids), place * PAIRS, 1).astype(BF)
    copies = [
        pltpu.make_async_copy(
            txt_pay, txt_all.at[d * TXT_ROWS : (d + 1) * TXT_ROWS, :], sems.at[d]
        )
        for d in range(16)
    ]
    for copy in copies:
        copy.start()
    for copy in copies:
        copy.wait()


def text_rows(*args):
    return pl.pallas_call(
        text_rows_kernel,
        out_shape=far(16 * TXT_ROWS, EMBED, BF),
        out_specs=loose(1)[0],
        scratch_shapes=[
            pltpu.VMEM((8, EMBED), jnp.int32),
            pltpu.VMEM((TXT_ROWS, EMBED), BF),
            pltpu.SemaphoreType.DMA((16,)),
        ],
        compiler_params=params(4),
        cost_estimate=cost(1.0),
        name="text_rows",
    )(*from_far(*args))


def front_kernel(img, img_ids, block_in, taps, gain, bias, blk, means, mixed, ids):
    blk[IMG_AT : IMG_AT + PAIRS, :] = unit_rows(img[...].astype(F32))[0].astype(BF)
    blk[IMG_AT + PAIRS : ROWS, :] = id_rows(img_ids, ids).astype(BF)
    column = lax.broadcasted_iota(jnp.int32, (SIDE, 128), 0)

    def lanes(c, sums):
        at = pl.ds(pl.multiple_of(c * 128, 128), 128)
        patch = block_in[:, at].astype(F32)
        rows = [patch[r * SIDE : (r + 1) * SIDE] for r in range(SIDE)]
        total = rows[0]
        for r in range(1, SIDE):
            total = total + rows[r]
        mean = jnp.sum(total, axis=0, keepdims=True) / PATCHES
        means[0:1, at] = mean.astype(BF).astype(F32)
        acc = [jnp.zeros((SIDE, 128), F32) for _ in range(SIDE)]
        for across in range(KERNEL):
            move = across - KERNEL // 2
            if move == 0:
                moved = rows
            else:
                inside = (column + move >= 0) & (column + move < SIDE)
                moved = [
                    jnp.where(inside, pltpu.roll(row, (-move) % SIDE, 0), 0.0) for row in rows
                ]
            for above in range(KERNEL):
                tap = taps[above * KERNEL + across : above * KERNEL + across + 1, at]
                for r in range(SIDE):
                    source = r + above - KERNEL // 2
                    if 0 <= source < SIDE:
                        acc[r] = acc[r] + tap * moved[source]
        for r in range(SIDE):
            mixed[r * SIDE : (r + 1) * SIDE, at] = acc[r]
        return tuple(s + a for s, a in zip(sums, acc))

    sums = lax.fori_loop(
        0, WIDTH // 128, lanes, tuple(jnp.zeros((SIDE, 128), F32) for _ in range(SIDE))
    )
    centre = jnp.concatenate(
        [jnp.sum(s, axis=1, keepdims=True) / WIDTH for s in sums], axis=0
    )
    square = jnp.zeros((PATCHES, 128), F32)
    for c in range(WIDTH // 128):
        off = mixed[:, c * 128 : (c + 1) * 128] - centre
        square = square + off * off
    inverse = 1.0 / jnp.sqrt(jnp.sum(square, axis=1, keepdims=True) / WIDTH + 1e-06)
    for c in range(WIDTH // 128):
        at = slice(c * 128, (c + 1) * 128)
        normal = (mixed[:, at] - centre) * inverse
        seg, lane = divmod(c * 128, EMBED)
        blk[seg * PATCHES : (seg + 1) * PATCHES, lane : lane + 128] = (
            normal * gain[:, at] + bias[:, at]
        ).astype(BF)


def front(*args):
    return pl.pallas_call(
        front_kernel,
        out_shape=(near(ROWS, EMBED, BF), far(1, WIDTH, F32)),
        scratch_shapes=[
            pltpu.VMEM((PATCHES, WIDTH), F32),
            pltpu.VMEM((8, EMBED), jnp.int32),
        ],
        compiler_params=params(8),
        cost_estimate=cost(4.5),
        name="front",
    )(*from_far(*args))


def turn_into(blocks, turn):
    for seg in range(SEG):
        at = slice(seg * PATCHES, (seg + 1) * PATCHES)
        for p in range(len(blocks) // 2):
            rows = jnp.concatenate([b[at, :] for b in blocks[2 * p : 2 * p + 2]], axis=0)
            turn[seg * EMBED : (seg + 1) * EMBED, p * 128 : (p + 1) * 128] = jnp.transpose(rows)


def step_kernel(count, *refs):
    blocks, refs = refs[:count], refs[count:]
    w_up, texts, temp_log, logit_bias, *refs = refs
    outs, (sums, firsts), scratch, sems = refs[:4], refs[4:6], refs[6:10], refs[10]
    slope, image_part, weights, turn = scratch
    copies = [
        pltpu.make_async_copy(source, into, sems.at[i])
        for i, (source, into) in enumerate(zip(scratch, outs))
    ]
    turn_into(blocks, turn)
    copies[3].start()
    root = math.sqrt(2.0 / math.pi)
    hidden = None
    for seg in range(SEG):
        rows = jnp.concatenate(
            [b[seg * PATCHES : (seg + 1) * PATCHES, :] for b in blocks], axis=0
        )
        part = jnp.dot(
            rows, w_up[seg * EMBED : (seg + 1) * EMBED, :], preferred_element_type=F32
        )
        hidden = part if hidden is None else hidden + part
    square = hidden * hidden
    curve = jnp.tanh(root * (hidden + 0.044715 * (square * hidden)))
    half = 0.5 * (1.0 + curve)
    active = (hidden * half).astype(BF).astype(F32)
    slope[...] = half + 0.5 * hidden * (1.0 - curve * curve) * (
        root * (1.0 + 3.0 * 0.044715 * square)
    )
    copies[0].start()
    for i in range(count):
        sums[i : i + 1, :] = jnp.sum(
            active[i * PATCHES : (i + 1) * PATCHES], axis=0, keepdims=True
        )

    temper = jnp.exp(temp_log[...])
    text_rows = jnp.concatenate(
        [texts[d * TXT_ROWS : d * TXT_ROWS + PAIRS, :] for d in range(16)], axis=0
    )
    digits = texts[PAIRS : PAIRS + 8, 0:512].astype(F32)
    for d in range(1, 16):
        at = d * TXT_ROWS + PAIRS
        digits = digits + texts[at : at + 8, 0:512].astype(F32)
    text_ids = digits[0:1] * 128.0 + digits[1:2]
    columns = []
    for b in blocks:
        pair = b[IMG_AT + PAIRS : ROWS, 0:128].astype(F32)
        row = jnp.broadcast_to(pair[0:1] * 128.0 + pair[1:2], (128, 128))
        columns.append(jnp.transpose(row)[0:PAIRS, 0:1])
    image_ids = jnp.concatenate(columns, axis=0)
    images = jnp.concatenate([b[IMG_AT : IMG_AT + PAIRS, :] for b in blocks], axis=0)
    scores = lax.dot_general(
        images, text_rows, (((1,), (1,)), ((), ())), preferred_element_type=F32
    )
    logits = temper * scores + logit_bias[...]
    labels = jnp.where(image_ids == text_ids, 1.0, -1.0)
    weight = (temper * -labels * jax.nn.sigmoid(-labels * logits)).astype(BF)
    weights[...] = weight
    copies[2].start()
    image = jnp.dot(weight, text_rows, preferred_element_type=F32)
    image_part[...] = image.astype(BF)
    copies[1].start()
    for i in range(count):
        firsts[i : i + 1, :] = image[i * PAIRS : i * PAIRS + 1]
    for copy in copies:
        copy.wait()


def step(blocks, w_up, texts, temp_log, logit_bias):
    count = len(blocks)
    dims = [
        (count * PATCHES, HID, F32),
        (count * PAIRS, EMBED, BF),
        (count * PAIRS, 16 * PAIRS, BF),
        (WIDTH, count * PATCHES, BF),
    ]
    return pl.pallas_call(
        functools.partial(step_kernel, count),
        out_shape=(
            *(far(*dim) for dim in dims),
            near(count, HID, F32),
            near(count, EMBED, F32),
        ),
        in_specs=whole(count + 4),
        out_specs=(*loose(4), *whole(2)),
        scratch_shapes=[pltpu.VMEM(dim[:2], dim[2]) for dim in dims]
        + [pltpu.SemaphoreType.DMA((4,))],
        compiler_params=params(14),
        cost_estimate=cost(1.5 + 0.8 * count),
        name="step",
    )(*blocks, w_up, texts, temp_log, logit_bias)


def mean_kernel(*refs):
    count = UNITS
    sums, firsts = refs[:count], refs[count : 2 * count]
    w_down, out, total_out, held = refs[2 * count :]
    total = jnp.concatenate([s[...] for s in sums], axis=0)
    total_out[...] = total.astype(BF)
    mean = total / PATCHES
    first = mean.astype(BF)
    rest = mean - first.astype(F32)
    second = rest.astype(BF)
    third = (rest - second.astype(F32)).astype(BF)
    three = jnp.dot(
        jnp.concatenate([first, second, third], axis=0), w_down[...], preferred_element_type=F32
    )
    partial = three[0:16] + three[16:32] + three[32:48]
    rows = jnp.concatenate([f[...] for f in firsts], axis=0)
    for c in range(6):
        held[:, c, :] = partial[:, c * 512 : (c + 1) * 512]
    for c in range(2):
        held[:, 6 + c, :] = rows[:, c * 512 : (c + 1) * 512]
    for j, key in enumerate(KEYS):
        at = pl.ds(pl.multiple_of(absolute(key) * 8, 8), 8)
        out[at, :] = held[j].astype(BF)


def mean_rows(sums, firsts, w_down):
    return pl.pallas_call(
        mean_kernel,
        out_shape=(far(128, 512, BF), far(16, HID, BF)),
        in_specs=whole(2 * len(GROUPS) + 1),
        scratch_shapes=[pltpu.VMEM((16, 8, 512), F32)],
        compiler_params=params(6),
        cost_estimate=cost(0.8),
        name="mean_rows",
    )(*sums, *firsts, w_down)


def head_kernel(parts, means, scale, gain, bias, w_far, out, w_proj, sems):
    quarter = WIDTH // 4
    copies = [
        pltpu.make_async_copy(
            w_far.at[i * quarter : (i + 1) * quarter, :],
            w_proj.at[i * quarter : (i + 1) * quarter, :],
            sems.at[i],
        )
        for i in range(4)
    ]
    for copy in copies:
        copy.start()
    total = parts[0:8, :].astype(F32)
    for d in range(1, 16):
        total = total + parts[d * 8 : (d + 1) * 8, :].astype(F32)
    block_mean = jnp.concatenate([total[c : c + 1] for c in range(6)], axis=1)
    image_sum = jnp.concatenate([total[6:7], total[7:8]], axis=1)
    pooled = means[...] + scale[...] * block_mean
    centred = pooled - jnp.sum(pooled, axis=1, keepdims=True) / WIDTH
    inverse = 1.0 / jnp.sqrt(jnp.sum(centred * centred, axis=1, keepdims=True) / WIDTH + 1e-06)
    head_norm = centred * inverse
    head_out = jnp.broadcast_to(head_norm * gain[...] + bias[...], (8, WIDTH)).astype(BF)
    embed = None
    for i in range(4):
        at = slice(i * quarter, (i + 1) * quarter)
        copies[i].wait()
        piece = jnp.dot(head_out[:, at], w_proj[at, :], preferred_element_type=F32)
        embed = piece if embed is None else embed + piece
    embed = embed[0:1]
    unit, length = unit_rows(embed)
    inner = jnp.sum(unit * image_sum, axis=1, keepdims=True)
    embed_grad = jnp.broadcast_to((image_sum - unit * inner) / length, (8, EMBED)).astype(BF)
    head_grad = lax.dot_general(
        embed_grad, w_proj[...], (((1,), (1,)), ((), ())), preferred_element_type=F32
    )[0:1]
    norm_grad = head_grad * gain[...]
    pool_grad = inverse * (
        norm_grad
        - jnp.sum(norm_grad, axis=1, keepdims=True) / WIDTH
        - head_norm * (jnp.sum(norm_grad * head_norm, axis=1, keepdims=True) / WIDTH)
    )
    row = scale[...] * pool_grad / PATCHES
    tile = jnp.concatenate([row[:, c * HID : (c + 1) * HID] for c in range(8)], axis=0).astype(BF)
    for d in range(16):
        out[d * 8 : (d + 1) * 8, :] = tile


def head(parts, means, scale, gain, bias, w_proj):
    return pl.pallas_call(
        head_kernel,
        out_shape=far(128, HID, BF),
        in_specs=whole(5) + loose(1),
        scratch_shapes=[pltpu.VMEM((WIDTH, EMBED), BF), pltpu.SemaphoreType.DMA((4,))],
        compiler_params=params(14),
        cost_estimate=cost(5.0),
        name="head",
    )(parts, *from_far(means, scale, gain, bias, w_proj))


def text_kernel(*refs):
    blocks = refs[:16]
    weights, images = (refs[16 + i * UNITS : 16 + (i + 1) * UNITS] for i in range(2))
    txt_send, txt_keep, img_send, img_keep, rows, weight, image, sems = refs[16 + 2 * UNITS :]
    copies, first = [], 0
    for u, group in enumerate(GROUPS):
        at = slice(first, first + len(group) * PAIRS)
        first += len(group) * PAIRS
        copies.append(pltpu.make_async_copy(weights[u], weight.at[at, :], sems.at[2 * u]))
        copies.append(pltpu.make_async_copy(images[u], image.at[at, :], sems.at[2 * u + 1]))
    for i in range(16):
        at = slice(i * PAIRS, (i + 1) * PAIRS)
        source = blocks[i].at[IMG_AT : IMG_AT + PAIRS, :]
        copies.append(pltpu.make_async_copy(source, rows.at[at, :], sems.at[2 * UNITS + i]))
    for copy in copies:
        copy.start()
    for copy in copies:
        copy.wait()
    text_part = lax.dot_general(
        weight[...], rows[...], (((0,), (0,)), ((), ())), preferred_element_type=F32
    ).astype(BF)
    rows[...] = text_part
    high = lax.axis_index("x") >> 1
    for k in range(8):
        low, ylo, core = k >> 2, (k >> 1) & 1, k & 1
        at = slice(k * PAIRS, (k + 1) * PAIRS)
        for into, side in ((txt_keep, high), (txt_send, 1 - high)):
            first = (ylo * 8 + low * 2 + core + 4 * side) * PAIRS
            into[at, :] = rows[pl.ds(pl.multiple_of(first, PAIRS), PAIRS), :]

    z = lax.axis_index("z")
    for j, (offset, side) in enumerate(KEYS):
        owner = lax.rem(z + offset, NZ)
        place = (owner & 1) * 4 + (owner & 2) + (owner >> 2)
        at = pl.ds(pl.multiple_of(place * PAIRS, PAIRS), PAIRS)
        into = img_keep if side == 0 else img_send
        into[at, :] = image[j * PAIRS : (j + 1) * PAIRS, :]


def text_parts(blocks, weights, images):
    return pl.pallas_call(
        text_kernel,
        out_shape=(far(8 * PAIRS, EMBED, BF),) * 4,
        in_specs=loose(16 + 2 * UNITS),
        out_specs=tuple(whole(4)),
        scratch_shapes=[
            pltpu.VMEM((16 * PAIRS, EMBED), BF),
            pltpu.VMEM((16 * PAIRS, 16 * PAIRS), BF),
            pltpu.VMEM((16 * PAIRS, EMBED), BF),
            pltpu.SemaphoreType.DMA((16 + 2 * UNITS,)),
        ],
        compiler_params=params(14),
        cost_estimate=cost(3.8),
        name="text_parts",
    )(*from_far(*blocks, *weights, *images))


def halve_kernel(bits, *refs):
    keeps, gots, sends, outs = (refs[2 * i : 2 * i + 2] for i in range(4))
    for (axis, shift), first, second, send, keep in zip(bits, keeps, gots, sends, outs):
        mine = (lax.axis_index(axis) >> shift) & 1
        rows = send.shape[0]
        for into, part in ((keep, mine), (send, 1 - mine)):
            at = pl.ds(pl.multiple_of(part * rows, rows), rows)
            into[...] = (first[at, :].astype(F32) + second[at, :].astype(F32)).astype(BF)


def halved(bits, keeps, gots):
    outs = pl.pallas_call(
        functools.partial(halve_kernel, bits),
        out_shape=(far(keeps[0].shape[0] // 2, EMBED, BF),) * 4,
        in_specs=whole(4),
        compiler_params=params(8),
        cost_estimate=cost(1.5),
        name="halved",
    )(*from_far(*keeps), *gots)
    return outs[:2], outs[2:]


def partner(value, axis, length, bit):
    return lax.ppermute(value, axis, [(i, i ^ bit) for i in range(length)])


def back_kernel(*refs):
    grads, w_down, total = refs[:3]
    slopes, turns = refs[3 : 3 + UNITS], refs[3 + UNITS : 3 + 2 * UNITS]
    send, keep, held, wide, hid_grad, slope, rows, block, sems = refs[3 + 2 * UNITS :]
    slope_copies, low_copies, high_copies, first = [], [], [], 0
    low, high = slice(0, WIDTH // 2), slice(WIDTH // 2, WIDTH)
    for u, group in enumerate(GROUPS):
        at = slice(first, first + len(group) * PATCHES)
        first += len(group) * PATCHES
        slope_copies.append(pltpu.make_async_copy(slopes[u], slope.at[at, :], sems.at[3 * u]))
        for half, into, sem in ((low, low_copies, 1), (high, high_copies, 2)):
            into.append(
                pltpu.make_async_copy(
                    turns[u].at[half, :], rows.at[half, at], sems.at[3 * u + sem]
                )
            )
    for copy in (*slope_copies, *low_copies, *high_copies):
        copy.start()
    keep[8 * HALF :, :] = total[...]
    send[8 * HALF :, :] = total[...]
    for j, key in enumerate(KEYS):
        at = pl.ds(pl.multiple_of(absolute(key) * 8, 8), 8)
        held[j] = grads[at, :].astype(F32)
    for c in range(8):
        wide[:, c * HID : (c + 1) * HID] = held[:, c, :]
    row_down = lax.dot_general(
        wide[...].astype(BF), w_down[...], (((1,), (1,)), ((), ())), preferred_element_type=F32
    )
    for copy in slope_copies:
        copy.wait()
    for j in range(16):
        at = slice(j * PATCHES, (j + 1) * PATCHES)
        hid_grad[at, :] = (slope[at, :] * row_down[j : j + 1]).astype(BF)
    core = lax.axis_index("core")

    def slabs(k, carry):
        at = pl.ds(pl.multiple_of(k * 2 * SLAB, 128), 2 * SLAB)
        block[...] = jnp.dot(rows[at, :], hid_grad[...], preferred_element_type=F32).astype(BF)
        mine = wide[:, at]
        swapped = pltpu.roll(mine, SLAB, 1)
        to = pl.ds(pl.multiple_of(k * HALF, 16), SLAB)
        below = pl.ds(pl.multiple_of(k * HALF + SLAB, 16), 16)
        for into, side in ((keep, core), (send, 1 - core)):
            into[to, :] = block[pl.ds(pl.multiple_of(side * SLAB, SLAB), SLAB), :]
            into[below, :] = jnp.where(side == 0, mine, swapped).astype(BF)
        return carry

    for half, copies in enumerate((low_copies, high_copies)):
        for copy in copies:
            copy.wait()
        lax.fori_loop(half * 4, half * 4 + 4, slabs, 0)


def backward(grads, w_down, total, slopes, turns):
    return pl.pallas_call(
        back_kernel,
        out_shape=(near(8 * HALF + 16, HID, BF),) * 2,
        in_specs=whole(3) + loose(2 * UNITS),
        out_specs=tuple(whole(2)),
        scratch_shapes=[
            pltpu.VMEM((16, 8, HID), F32),
            pltpu.VMEM((16, WIDTH), F32),
            pltpu.VMEM((16 * PATCHES, HID), BF),
            pltpu.VMEM((16 * PATCHES, HID), F32),
            pltpu.VMEM((WIDTH, 16 * PATCHES), BF),
            pltpu.VMEM((2 * SLAB, HID), BF),
            pltpu.SemaphoreType.DMA((3 * UNITS,)),
        ],
        compiler_params=params(16),
        cost_estimate=cost(6.5),
        name="backward",
    )(grads, w_down, *from_far(total, *slopes, *turns))


def join_kernel(keep, got, out):
    lane = lax.broadcasted_iota(jnp.int32, (16, HID), 1)
    for k in range(8):
        at = slice(k * HALF, k * HALF + SLAB)
        below = slice(k * HALF + SLAB, (k + 1) * HALF)
        to = k * FULL
        out[to : to + SLAB, :] = (keep[at, :].astype(F32) + got[at, :].astype(F32)).astype(BF)
        other = pltpu.roll(got[below, :].astype(F32), SLAB, 1)
        out[to + SLAB : to + HALF, :] = jnp.where(
            lane < SLAB, keep[below, :].astype(F32), other
        ).astype(BF)
        out[to + HALF : to + HALF + 16, :] = keep[8 * HALF :, :]
        out[to + HALF + 16 : to + FULL, :] = got[8 * HALF :, :]


def join(keep, got):
    return pl.pallas_call(
        join_kernel,
        out_shape=far(8 * FULL, HID, BF),
        in_specs=whole(2),
        compiler_params=params(12),
        cost_estimate=cost(1.0),
        name="join",
    )(keep, got)


def last_kernel(got, up_out, down_out):
    total = got[0:SLAB, :].astype(F32)
    for k in range(1, 8):
        total = total + got[k * FULL : k * FULL + SLAB, :].astype(F32)
    up_out[...] = total
    grads = jnp.concatenate(
        [got[k * FULL + SLAB : k * FULL + HALF, :] for k in range(8)], axis=0
    )
    others = pltpu.roll(grads.astype(F32), SLAB, 1).astype(BF)
    down = None
    for side, left in enumerate((grads, others)):
        right = jnp.concatenate(
            [
                got[k * FULL + HALF + side * 16 : k * FULL + HALF + side * 16 + 16, :]
                for k in range(8)
            ],
            axis=0,
        )
        part = lax.dot_general(
            left, right, (((0,), (0,)), ((), ())), preferred_element_type=F32
        )
        down = part if down is None else down + part
    down_out[...] = down[0:SLAB, :]


def last(got):
    return pl.pallas_call(
        last_kernel,
        out_shape=(far(SLAB, HID, F32), far(SLAB, HID, F32)),
        in_specs=whole(1),
        compiler_params=params(12),
        cost_estimate=cost(2.0),
        name="last",
    )(got)


def rows_kernel(count, *refs):
    emb, out = refs[count:]
    total = None
    for ref in refs[:count]:
        for d in range(ref.shape[0] // PAIRS):
            part = ref[d * PAIRS : (d + 1) * PAIRS, :].astype(F32)
            total = part if total is None else total + part
    unit, length = unit_rows(emb[...].astype(F32))
    inner = jnp.sum(unit * total, axis=1, keepdims=True)
    out[...] = (total - unit * inner) / length


def row_grads(parts, emb, name):
    return pl.pallas_call(
        functools.partial(rows_kernel, len(parts)),
        out_shape=far(PAIRS, EMBED, F32),
        compiler_params=params(8),
        cost_estimate=cost(0.9),
        name=name,
    )(*parts, *from_far(emb))


def swap(value, axes, count):
    rows, columns = value.shape
    parts = value.reshape(count, rows // count, columns)
    return lax.all_to_all(parts, axes, 0, 0, tiled=True).reshape(rows, columns)


def on_device(
    img_emb,
    txt_emb,
    img_ids,
    txt_ids,
    temp_log,
    logit_bias,
    block_in,
    dw_kernel,
    ln_gain,
    ln_bias,
    w_up,
    w_down,
    layer_scale,
    head_gain,
    head_bias,
    w_proj,
):
    texts = swap(text_rows(txt_emb, txt_ids.reshape(1, PAIRS)), DP, 16)
    blk, means = front(
        img_emb,
        img_ids.reshape(1, PAIRS),
        block_in,
        dw_kernel,
        ln_gain.reshape(1, WIDTH),
        ln_bias.reshape(1, WIDTH),
    )
    temper = temp_log.reshape(1, 1)
    offset = logit_bias.reshape(1, 1)
    got = {(0, 0): blk}
    kept = []

    def send_on(side, distance, up=True, down=True):
        if up:
            got[NZ - distance, side] = hop(got[(NZ - distance + 1) % NZ, side], "z", NZ, 1)
        if down:
            got[distance, side] = hop(got[distance - 1, side], "z", NZ, -1)

    def tie(keys, *values):
        tied = lax.optimization_barrier((*(got[key] for key in keys), *values))
        got.update(zip(keys, tied))
        return tied[len(keys) :]

    def work(unit):
        return step([got[key] for key in GROUPS[unit]], w_up, texts, temper, offset)

    got[0, 1] = hop(blk, "yhi", 2, 1)
    send_on(0, 1)
    tie([(NZ - 1, 0), (1, 0)])
    send_on(1, 1)
    send_on(0, 2)
    send_on(1, 2)
    send_on(0, 3)
    kept.append(tie([(NZ - 2, 1)], *work(0)))
    send_on(1, 3)
    send_on(0, NZ // 2, down=False)
    kept.append(tie([(3, 1)], *work(1)))
    send_on(1, NZ // 2, up=False)
    kept += [work(unit) for unit in range(2, UNITS)]

    slopes, images, weights, turns, sums, firsts = zip(*kept)
    means_out, total = mean_rows(sums, firsts, w_down)
    means_out, *weights = lax.optimization_barrier((means_out, *weights))
    parts = swap(means_out, FSDP, 16)
    sends = text_parts([got[key] for key in KEYS], weights, images)
    parts, txt_send, txt_keep, img_send, img_keep = lax.optimization_barrier((parts, *sends))
    txt_got = partner(txt_send, "x", 4, 2)
    img_got = hop(img_send, "yhi", 2, 1)
    grads = head(
        parts,
        means,
        layer_scale.reshape(1, WIDTH),
        head_gain.reshape(1, WIDTH),
        head_bias.reshape(1, WIDTH),
        w_proj,
    )
    grads = swap(grads, FSDP, 16)
    sends, keeps = halved((("x", 0), ("z", 0)), (txt_keep, img_keep), (txt_got, img_got))
    grads, *sends = lax.optimization_barrier((grads, *sends))
    gots = (partner(sends[0], "x", 4, 1), partner(sends[1], "z", NZ, 1))
    send, keep = backward(grads, w_down, total, slopes, turns)
    send, *gots = lax.optimization_barrier((send, *gots))
    got_core = hop(send, "core", 2, 1)
    sends, keeps = halved((("ylo", 0), ("z", 1)), keeps, gots)
    gots = (partner(sends[0], "ylo", 2, 1), partner(sends[1], "z", NZ, 2))
    both = join(keep, got_core)
    both, *gots = lax.optimization_barrier((both, *gots))
    sends, keeps = halved((("core", 0), ("z", 2)), keeps, gots)
    w_up_grad, w_down_grad = last(swap(both, ("ylo", "x"), 8))
    w_down_grad = w_down_grad.T
    txt_grad = row_grads((keeps[0], partner(sends[0], "core", 2, 1)), txt_emb, "txt_rows")
    img_grad = row_grads((keeps[1], partner(sends[1], "z", NZ, 4)), img_emb, "img_rows")
    return (img_grad, txt_grad, w_up_grad, w_down_grad)


def solution(mesh):
    split = Mesh(mesh.devices.reshape(2, 4, 2, NZ, 2), ALL)
    in_specs = (
        P(ALL, None),
        P(ALL, None),
        P(ALL),
        P(ALL),
        P(),
        P(),
        P(ALL, None),
        P(),
        P(),
        P(),
        P(None, FSDP),
        P(FSDP, None),
        P(),
        P(),
        P(),
        P(),
    )
    out_specs = (P(ALL, None), P(ALL, None), P(DP, FSDP), P(FSDP, DP))
    return jax.shard_map(
        on_device, mesh=split, in_specs=in_specs, out_specs=out_specs, check_vma=False
    )
```

```python
import functools
import math

import jax
import jax.numpy as jnp
from jax import lax
from jax.experimental import pallas as pl
from jax.experimental.pallas import tpu as pltpu
from jax.sharding import Mesh
from jax.sharding import PartitionSpec as P

KERNEL = 7
SIDE = 8
PATCHES = SIDE * SIDE
DP = ("ylo", "x", "core")
FSDP = ("z", "yhi")
ALL = DP + FSDP
NZ = 8
PAIRS = 32
EMBED = 1024
WIDTH = 3072
HID = 384
SEG = WIDTH // EMBED
IMG_AT = SEG * PATCHES
ROWS = IMG_AT + PAIRS + 8
TXT_ROWS = PAIRS + 8
SLAB = WIDTH // 16
HALF = SLAB + 16
FULL = HALF + 32
BF = jnp.bfloat16
F32 = jnp.float32

GROUPS = [[(0, 0), (0, 1)]]
for _step in range(1, NZ // 2):
    GROUPS.append([(NZ - _step, 0), (NZ - _step, 1), (_step, 0), (_step, 1)])
GROUPS.append([(NZ // 2, 0), (NZ // 2, 1)])
KEYS = [key for group in GROUPS for key in group]
UNITS = len(GROUPS)


def params(mib):
    return pltpu.CompilerParams(vmem_limit_bytes=mib << 20)


def cost(micros):
    return pl.CostEstimate(flops=0, transcendentals=0, bytes_accessed=int(micros * 3_690_000))


def whole(count):
    return [pl.BlockSpec(memory_space=pltpu.VMEM)] * count


def loose(count):
    return [pl.BlockSpec(memory_space=pl.ANY)] * count


def near(rows, columns, dtype):
    return jax.ShapeDtypeStruct((rows, columns), dtype)


def far(rows, columns, dtype):
    return pltpu.HBM((rows, columns), dtype)


def from_far(*arrays):
    return [pltpu.with_memory_space_constraint(array, pltpu.HBM) for array in arrays]


def hop(value, axis, length, step):
    return lax.ppermute(value, axis, [(i, (i + step) % length) for i in range(length)])


def absolute(key):
    z = lax.rem(lax.axis_index("z") + key[0], NZ)
    y = lax.axis_index("yhi")
    return z * 2 + (y if key[1] == 0 else 1 - y)


def unit_rows(values):
    length = jnp.sqrt(jnp.sum(values * values, axis=1, keepdims=True) + 1e-06)
    return (values / length, length)


def id_rows(source, ids):
    ids[...] = jnp.zeros_like(ids)
    ids[0:1, 0:PAIRS] = source[...]
    row = lax.broadcasted_iota(jnp.int32, (8, EMBED), 0)
    value = jnp.broadcast_to(ids[0:1, :], (8, EMBED))
    return jnp.where(row == 0, value >> 7, jnp.where(row == 1, value & 127, 0)).astype(F32)


def front_kernel(
    img, txt, img_ids, txt_ids, block_in, taps, gain, bias, blk, txt_all, means, mixed, ids, txt_pay, sems
):
    txt_pay[0:PAIRS, :] = unit_rows(txt[...].astype(F32))[0].astype(BF)
    place = (lax.axis_index("ylo") * 4 + lax.axis_index("x")) * 2 + lax.axis_index("core")
    txt_pay[PAIRS:TXT_ROWS, :] = pltpu.roll(id_rows(txt_ids, ids), place * PAIRS, 1).astype(BF)
    copies = [
        pltpu.make_async_copy(
            txt_pay, txt_all.at[d * TXT_ROWS : (d + 1) * TXT_ROWS, :], sems.at[d]
        )
        for d in range(16)
    ]
    for copy in copies:
        copy.start()
    blk[IMG_AT : IMG_AT + PAIRS, :] = unit_rows(img[...].astype(F32))[0].astype(BF)
    blk[IMG_AT + PAIRS : ROWS, :] = id_rows(img_ids, ids).astype(BF)
    column = lax.broadcasted_iota(jnp.int32, (SIDE, 128), 0)

    def lanes(c, sums):
        at = pl.ds(pl.multiple_of(c * 128, 128), 128)
        patch = block_in[:, at].astype(F32)
        rows = [patch[r * SIDE : (r + 1) * SIDE] for r in range(SIDE)]
        total = rows[0]
        for r in range(1, SIDE):
            total = total + rows[r]
        mean = jnp.sum(total, axis=0, keepdims=True) / PATCHES
        means[0:1, at] = mean.astype(BF).astype(F32)
        acc = [jnp.zeros((SIDE, 128), F32) for _ in range(SIDE)]
        for across in range(KERNEL):
            move = across - KERNEL // 2
            if move == 0:
                moved = rows
            else:
                inside = (column + move >= 0) & (column + move < SIDE)
                moved = [
                    jnp.where(inside, pltpu.roll(row, (-move) % SIDE, 0), 0.0) for row in rows
                ]
            for above in range(KERNEL):
                tap = taps[above * KERNEL + across : above * KERNEL + across + 1, at]
                for r in range(SIDE):
                    source = r + above - KERNEL // 2
                    if 0 <= source < SIDE:
                        acc[r] = acc[r] + tap * moved[source]
        for r in range(SIDE):
            mixed[r * SIDE : (r + 1) * SIDE, at] = acc[r]
        return tuple(s + a for s, a in zip(sums, acc))

    sums = lax.fori_loop(
        0, WIDTH // 128, lanes, tuple(jnp.zeros((SIDE, 128), F32) for _ in range(SIDE))
    )
    centre = jnp.concatenate(
        [jnp.sum(s, axis=1, keepdims=True) / WIDTH for s in sums], axis=0
    )
    square = jnp.zeros((PATCHES, 128), F32)
    for c in range(WIDTH // 128):
        off = mixed[:, c * 128 : (c + 1) * 128] - centre
        square = square + off * off
    inverse = 1.0 / jnp.sqrt(jnp.sum(square, axis=1, keepdims=True) / WIDTH + 1e-06)
    for c in range(WIDTH // 128):
        at = slice(c * 128, (c + 1) * 128)
        normal = (mixed[:, at] - centre) * inverse
        seg, lane = divmod(c * 128, EMBED)
        blk[seg * PATCHES : (seg + 1) * PATCHES, lane : lane + 128] = (
            normal * gain[:, at] + bias[:, at]
        ).astype(BF)
    for copy in copies:
        copy.wait()


def front(*args):
    return pl.pallas_call(
        front_kernel,
        out_shape=(
            near(ROWS, EMBED, BF),
            far(16 * TXT_ROWS, EMBED, BF),
            far(1, WIDTH, F32),
        ),
        out_specs=(pl.BlockSpec(), *loose(1), pl.BlockSpec()),
        scratch_shapes=[
            pltpu.VMEM((PATCHES, WIDTH), F32),
            pltpu.VMEM((8, EMBED), jnp.int32),
            pltpu.VMEM((TXT_ROWS, EMBED), BF),
            pltpu.SemaphoreType.DMA((16,)),
        ],
        compiler_params=params(8),
        cost_estimate=cost(4.5),
        name="front",
    )(*from_far(*args))


def turn_into(blocks, turn):
    for seg in range(SEG):
        at = slice(seg * PATCHES, (seg + 1) * PATCHES)
        for p in range(len(blocks) // 2):
            rows = jnp.concatenate([b[at, :] for b in blocks[2 * p : 2 * p + 2]], axis=0)
            turn[seg * EMBED : (seg + 1) * EMBED, p * 128 : (p + 1) * 128] = jnp.transpose(rows)


def step_kernel(count, *refs):
    blocks, refs = refs[:count], refs[count:]
    w_up, texts, temp_log, logit_bias, *refs = refs
    outs, (sums, firsts), scratch, sems = refs[:4], refs[4:6], refs[6:10], refs[10]
    slope, image_part, weights, turn = scratch
    copies = [
        pltpu.make_async_copy(source, into, sems.at[i])
        for i, (source, into) in enumerate(zip(scratch, outs))
    ]
    turn_into(blocks, turn)
    copies[3].start()
    root = math.sqrt(2.0 / math.pi)
    hidden = None
    for seg in range(SEG):
        rows = jnp.concatenate(
            [b[seg * PATCHES : (seg + 1) * PATCHES, :] for b in blocks], axis=0
        )
        part = jnp.dot(
            rows, w_up[seg * EMBED : (seg + 1) * EMBED, :], preferred_element_type=F32
        )
        hidden = part if hidden is None else hidden + part
    square = hidden * hidden
    curve = jnp.tanh(root * (hidden + 0.044715 * (square * hidden)))
    half = 0.5 * (1.0 + curve)
    active = (hidden * half).astype(BF).astype(F32)
    slope[...] = half + 0.5 * hidden * (1.0 - curve * curve) * (
        root * (1.0 + 3.0 * 0.044715 * square)
    )
    copies[0].start()
    for i in range(count):
        sums[i : i + 1, :] = jnp.sum(
            active[i * PATCHES : (i + 1) * PATCHES], axis=0, keepdims=True
        )

    temper = jnp.exp(temp_log[...])
    text_rows = jnp.concatenate(
        [texts[d * TXT_ROWS : d * TXT_ROWS + PAIRS, :] for d in range(16)], axis=0
    )
    digits = texts[PAIRS : PAIRS + 8, 0:512].astype(F32)
    for d in range(1, 16):
        at = d * TXT_ROWS + PAIRS
        digits = digits + texts[at : at + 8, 0:512].astype(F32)
    text_ids = digits[0:1] * 128.0 + digits[1:2]
    columns = []
    for b in blocks:
        pair = b[IMG_AT + PAIRS : ROWS, 0:128].astype(F32)
        row = jnp.broadcast_to(pair[0:1] * 128.0 + pair[1:2], (128, 128))
        columns.append(jnp.transpose(row)[0:PAIRS, 0:1])
    image_ids = jnp.concatenate(columns, axis=0)
    images = jnp.concatenate([b[IMG_AT : IMG_AT + PAIRS, :] for b in blocks], axis=0)
    scores = lax.dot_general(
        images, text_rows, (((1,), (1,)), ((), ())), preferred_element_type=F32
    )
    logits = temper * scores + logit_bias[...]
    labels = jnp.where(image_ids == text_ids, 1.0, -1.0)
    weight = (temper * -labels * jax.nn.sigmoid(-labels * logits)).astype(BF)
    weights[...] = weight
    copies[2].start()
    image = jnp.dot(weight, text_rows, preferred_element_type=F32)
    image_part[...] = image.astype(BF)
    copies[1].start()
    for i in range(count):
        firsts[i : i + 1, :] = image[i * PAIRS : i * PAIRS + 1]
    for copy in copies:
        copy.wait()


def step(blocks, w_up, texts, temp_log, logit_bias):
    count = len(blocks)
    dims = [
        (count * PATCHES, HID, F32),
        (count * PAIRS, EMBED, BF),
        (count * PAIRS, 16 * PAIRS, BF),
        (WIDTH, count * PATCHES, BF),
    ]
    return pl.pallas_call(
        functools.partial(step_kernel, count),
        out_shape=(
            *(far(*dim) for dim in dims),
            near(count, HID, F32),
            near(count, EMBED, F32),
        ),
        in_specs=whole(count + 4),
        out_specs=(*loose(4), *whole(2)),
        scratch_shapes=[pltpu.VMEM(dim[:2], dim[2]) for dim in dims]
        + [pltpu.SemaphoreType.DMA((4,))],
        compiler_params=params(14),
        cost_estimate=cost(1.5 + 0.8 * count),
        name="step",
    )(*blocks, w_up, texts, temp_log, logit_bias)


def mean_kernel(*refs):
    count = UNITS
    sums, firsts = refs[:count], refs[count : 2 * count]
    w_down, out, total_out, held = refs[2 * count :]
    total = jnp.concatenate([s[...] for s in sums], axis=0)
    total_out[...] = total.astype(BF)
    mean = total / PATCHES
    first = mean.astype(BF)
    rest = mean - first.astype(F32)
    second = rest.astype(BF)
    third = (rest - second.astype(F32)).astype(BF)
    three = jnp.dot(
        jnp.concatenate([first, second, third], axis=0), w_down[...], preferred_element_type=F32
    )
    partial = three[0:16] + three[16:32] + three[32:48]
    rows = jnp.concatenate([f[...] for f in firsts], axis=0)
    for c in range(6):
        held[:, c, :] = partial[:, c * 512 : (c + 1) * 512]
    for c in range(2):
        held[:, 6 + c, :] = rows[:, c * 512 : (c + 1) * 512]
    for j, key in enumerate(KEYS):
        at = pl.ds(pl.multiple_of(absolute(key) * 8, 8), 8)
        out[at, :] = held[j].astype(BF)


def mean_rows(sums, firsts, w_down):
    return pl.pallas_call(
        mean_kernel,
        out_shape=(far(128, 512, BF), far(16, HID, BF)),
        in_specs=whole(2 * len(GROUPS) + 1),
        scratch_shapes=[pltpu.VMEM((16, 8, 512), F32)],
        compiler_params=params(6),
        cost_estimate=cost(0.8),
        name="mean_rows",
    )(*sums, *firsts, w_down)


def head_kernel(parts, means, scale, gain, bias, w_far, out, w_proj, sems):
    quarter = WIDTH // 4
    copies = [
        pltpu.make_async_copy(
            w_far.at[i * quarter : (i + 1) * quarter, :],
            w_proj.at[i * quarter : (i + 1) * quarter, :],
            sems.at[i],
        )
        for i in range(4)
    ]
    for copy in copies:
        copy.start()
    total = parts[0:8, :].astype(F32)
    for d in range(1, 16):
        total = total + parts[d * 8 : (d + 1) * 8, :].astype(F32)
    block_mean = jnp.concatenate([total[c : c + 1] for c in range(6)], axis=1)
    image_sum = jnp.concatenate([total[6:7], total[7:8]], axis=1)
    pooled = means[...] + scale[...] * block_mean
    centred = pooled - jnp.sum(pooled, axis=1, keepdims=True) / WIDTH
    inverse = 1.0 / jnp.sqrt(jnp.sum(centred * centred, axis=1, keepdims=True) / WIDTH + 1e-06)
    head_norm = centred * inverse
    head_out = jnp.broadcast_to(head_norm * gain[...] + bias[...], (8, WIDTH)).astype(BF)
    embed = None
    for i in range(4):
        at = slice(i * quarter, (i + 1) * quarter)
        copies[i].wait()
        piece = jnp.dot(head_out[:, at], w_proj[at, :], preferred_element_type=F32)
        embed = piece if embed is None else embed + piece
    embed = embed[0:1]
    unit, length = unit_rows(embed)
    inner = jnp.sum(unit * image_sum, axis=1, keepdims=True)
    embed_grad = jnp.broadcast_to((image_sum - unit * inner) / length, (8, EMBED)).astype(BF)
    head_grad = lax.dot_general(
        embed_grad, w_proj[...], (((1,), (1,)), ((), ())), preferred_element_type=F32
    )[0:1]
    norm_grad = head_grad * gain[...]
    pool_grad = inverse * (
        norm_grad
        - jnp.sum(norm_grad, axis=1, keepdims=True) / WIDTH
        - head_norm * (jnp.sum(norm_grad * head_norm, axis=1, keepdims=True) / WIDTH)
    )
    row = scale[...] * pool_grad / PATCHES
    tile = jnp.concatenate([row[:, c * HID : (c + 1) * HID] for c in range(8)], axis=0).astype(BF)
    for d in range(16):
        out[d * 8 : (d + 1) * 8, :] = tile


def head(parts, means, scale, gain, bias, w_proj):
    return pl.pallas_call(
        head_kernel,
        out_shape=far(128, HID, BF),
        in_specs=whole(5) + loose(1),
        scratch_shapes=[pltpu.VMEM((WIDTH, EMBED), BF), pltpu.SemaphoreType.DMA((4,))],
        compiler_params=params(14),
        cost_estimate=cost(5.0),
        name="head",
    )(parts, *from_far(means, scale, gain, bias, w_proj))


def text_kernel(*refs):
    blocks = refs[:16]
    weights, images = (refs[16 + i * UNITS : 16 + (i + 1) * UNITS] for i in range(2))
    txt_send, txt_keep, img_send, img_keep, rows, weight, image, sems = refs[16 + 2 * UNITS :]
    copies, first = [], 0
    for u, group in enumerate(GROUPS):
        at = slice(first, first + len(group) * PAIRS)
        first += len(group) * PAIRS
        copies.append(pltpu.make_async_copy(weights[u], weight.at[at, :], sems.at[2 * u]))
        copies.append(pltpu.make_async_copy(images[u], image.at[at, :], sems.at[2 * u + 1]))
    for i in range(16):
        at = slice(i * PAIRS, (i + 1) * PAIRS)
        source = blocks[i].at[IMG_AT : IMG_AT + PAIRS, :]
        copies.append(pltpu.make_async_copy(source, rows.at[at, :], sems.at[2 * UNITS + i]))
    for copy in copies:
        copy.start()
    for copy in copies:
        copy.wait()
    text_part = lax.dot_general(
        weight[...], rows[...], (((0,), (0,)), ((), ())), preferred_element_type=F32
    ).astype(BF)
    rows[...] = text_part
    high = lax.axis_index("x") >> 1
    for k in range(8):
        low, ylo, core = k >> 2, (k >> 1) & 1, k & 1
        at = slice(k * PAIRS, (k + 1) * PAIRS)
        for into, side in ((txt_keep, high), (txt_send, 1 - high)):
            first = (ylo * 8 + low * 2 + core + 4 * side) * PAIRS
            into[at, :] = rows[pl.ds(pl.multiple_of(first, PAIRS), PAIRS), :]

    z = lax.axis_index("z")
    for j, (offset, side) in enumerate(KEYS):
        owner = lax.rem(z + offset, NZ)
        place = (owner & 1) * 4 + (owner & 2) + (owner >> 2)
        at = pl.ds(pl.multiple_of(place * PAIRS, PAIRS), PAIRS)
        into = img_keep if side == 0 else img_send
        into[at, :] = image[j * PAIRS : (j + 1) * PAIRS, :]


def text_parts(blocks, weights, images):
    return pl.pallas_call(
        text_kernel,
        out_shape=(far(8 * PAIRS, EMBED, BF),) * 4,
        in_specs=loose(16 + 2 * UNITS),
        out_specs=tuple(whole(4)),
        scratch_shapes=[
            pltpu.VMEM((16 * PAIRS, EMBED), BF),
            pltpu.VMEM((16 * PAIRS, 16 * PAIRS), BF),
            pltpu.VMEM((16 * PAIRS, EMBED), BF),
            pltpu.SemaphoreType.DMA((16 + 2 * UNITS,)),
        ],
        compiler_params=params(14),
        cost_estimate=cost(3.8),
        name="text_parts",
    )(*from_far(*blocks, *weights, *images))


def halve_kernel(bits, *refs):
    keeps, gots, sends, outs = (refs[2 * i : 2 * i + 2] for i in range(4))
    for (axis, shift), first, second, send, keep in zip(bits, keeps, gots, sends, outs):
        mine = (lax.axis_index(axis) >> shift) & 1
        rows = send.shape[0]
        for into, part in ((keep, mine), (send, 1 - mine)):
            at = pl.ds(pl.multiple_of(part * rows, rows), rows)
            into[...] = (first[at, :].astype(F32) + second[at, :].astype(F32)).astype(BF)


def halved(bits, keeps, gots):
    outs = pl.pallas_call(
        functools.partial(halve_kernel, bits),
        out_shape=(far(keeps[0].shape[0] // 2, EMBED, BF),) * 4,
        in_specs=whole(4),
        compiler_params=params(8),
        cost_estimate=cost(1.5),
        name="halved",
    )(*from_far(*keeps), *gots)
    return outs[:2], outs[2:]


def partner(value, axis, length, bit):
    return lax.ppermute(value, axis, [(i, i ^ bit) for i in range(length)])


def back_kernel(*refs):
    grads, w_down, total = refs[:3]
    slopes, turns = refs[3 : 3 + UNITS], refs[3 + UNITS : 3 + 2 * UNITS]
    send, keep, held, wide, hid_grad, slope, rows, block, sems = refs[3 + 2 * UNITS :]
    slope_copies, low_copies, high_copies, first = [], [], [], 0
    low, high = slice(0, WIDTH // 2), slice(WIDTH // 2, WIDTH)
    for u, group in enumerate(GROUPS):
        at = slice(first, first + len(group) * PATCHES)
        first += len(group) * PATCHES
        slope_copies.append(pltpu.make_async_copy(slopes[u], slope.at[at, :], sems.at[3 * u]))
        for half, into, sem in ((low, low_copies, 1), (high, high_copies, 2)):
            into.append(
                pltpu.make_async_copy(
                    turns[u].at[half, :], rows.at[half, at], sems.at[3 * u + sem]
                )
            )
    for copy in (*slope_copies, *low_copies, *high_copies):
        copy.start()
    keep[8 * HALF :, :] = total[...]
    send[8 * HALF :, :] = total[...]
    for j, key in enumerate(KEYS):
        at = pl.ds(pl.multiple_of(absolute(key) * 8, 8), 8)
        held[j] = grads[at, :].astype(F32)
    for c in range(8):
        wide[:, c * HID : (c + 1) * HID] = held[:, c, :]
    row_down = lax.dot_general(
        wide[...].astype(BF), w_down[...], (((1,), (1,)), ((), ())), preferred_element_type=F32
    )
    for copy in slope_copies:
        copy.wait()
    for j in range(16):
        at = slice(j * PATCHES, (j + 1) * PATCHES)
        hid_grad[at, :] = (slope[at, :] * row_down[j : j + 1]).astype(BF)
    core = lax.axis_index("core")

    def slabs(k, carry):
        at = pl.ds(pl.multiple_of(k * 2 * SLAB, 128), 2 * SLAB)
        block[...] = jnp.dot(rows[at, :], hid_grad[...], preferred_element_type=F32).astype(BF)
        mine = wide[:, at]
        swapped = pltpu.roll(mine, SLAB, 1)
        to = pl.ds(pl.multiple_of(k * HALF, 16), SLAB)
        below = pl.ds(pl.multiple_of(k * HALF + SLAB, 16), 16)
        for into, side in ((keep, core), (send, 1 - core)):
            into[to, :] = block[pl.ds(pl.multiple_of(side * SLAB, SLAB), SLAB), :]
            into[below, :] = jnp.where(side == 0, mine, swapped).astype(BF)
        return carry

    for half, copies in enumerate((low_copies, high_copies)):
        for copy in copies:
            copy.wait()
        lax.fori_loop(half * 4, half * 4 + 4, slabs, 0)


def backward(grads, w_down, total, slopes, turns):
    return pl.pallas_call(
        back_kernel,
        out_shape=(near(8 * HALF + 16, HID, BF),) * 2,
        in_specs=whole(3) + loose(2 * UNITS),
        out_specs=tuple(whole(2)),
        scratch_shapes=[
            pltpu.VMEM((16, 8, HID), F32),
            pltpu.VMEM((16, WIDTH), F32),
            pltpu.VMEM((16 * PATCHES, HID), BF),
            pltpu.VMEM((16 * PATCHES, HID), F32),
            pltpu.VMEM((WIDTH, 16 * PATCHES), BF),
            pltpu.VMEM((2 * SLAB, HID), BF),
            pltpu.SemaphoreType.DMA((3 * UNITS,)),
        ],
        compiler_params=params(16),
        cost_estimate=cost(6.5),
        name="backward",
    )(grads, w_down, *from_far(total, *slopes, *turns))


def join_kernel(keep, got, out):
    lane = lax.broadcasted_iota(jnp.int32, (16, HID), 1)
    for k in range(8):
        at = slice(k * HALF, k * HALF + SLAB)
        below = slice(k * HALF + SLAB, (k + 1) * HALF)
        to = k * FULL
        out[to : to + SLAB, :] = (keep[at, :].astype(F32) + got[at, :].astype(F32)).astype(BF)
        other = pltpu.roll(got[below, :].astype(F32), SLAB, 1)
        out[to + SLAB : to + HALF, :] = jnp.where(
            lane < SLAB, keep[below, :].astype(F32), other
        ).astype(BF)
        out[to + HALF : to + HALF + 16, :] = keep[8 * HALF :, :]
        out[to + HALF + 16 : to + FULL, :] = got[8 * HALF :, :]


def join(keep, got):
    return pl.pallas_call(
        join_kernel,
        out_shape=far(8 * FULL, HID, BF),
        in_specs=whole(2),
        compiler_params=params(12),
        cost_estimate=cost(1.0),
        name="join",
    )(keep, got)


def last_kernel(got, up_out, down_out):
    total = got[0:SLAB, :].astype(F32)
    for k in range(1, 8):
        total = total + got[k * FULL : k * FULL + SLAB, :].astype(F32)
    up_out[...] = total
    grads = jnp.concatenate(
        [got[k * FULL + SLAB : k * FULL + HALF, :] for k in range(8)], axis=0
    )
    others = pltpu.roll(grads.astype(F32), SLAB, 1).astype(BF)
    down = None
    for side, left in enumerate((grads, others)):
        right = jnp.concatenate(
            [
                got[k * FULL + HALF + side * 16 : k * FULL + HALF + side * 16 + 16, :]
                for k in range(8)
            ],
            axis=0,
        )
        part = lax.dot_general(
            left, right, (((0,), (0,)), ((), ())), preferred_element_type=F32
        )
        down = part if down is None else down + part
    down_out[...] = down[0:SLAB, :]


def last(got):
    return pl.pallas_call(
        last_kernel,
        out_shape=(far(SLAB, HID, F32), far(SLAB, HID, F32)),
        in_specs=whole(1),
        compiler_params=params(12),
        cost_estimate=cost(2.0),
        name="last",
    )(got)


def rows_kernel(count, *refs):
    emb, out = refs[count:]
    total = None
    for ref in refs[:count]:
        for d in range(ref.shape[0] // PAIRS):
            part = ref[d * PAIRS : (d + 1) * PAIRS, :].astype(F32)
            total = part if total is None else total + part
    unit, length = unit_rows(emb[...].astype(F32))
    inner = jnp.sum(unit * total, axis=1, keepdims=True)
    out[...] = (total - unit * inner) / length


def row_grads(parts, emb, name):
    return pl.pallas_call(
        functools.partial(rows_kernel, len(parts)),
        out_shape=far(PAIRS, EMBED, F32),
        compiler_params=params(8),
        cost_estimate=cost(0.9),
        name=name,
    )(*parts, *from_far(emb))


def swap(value, axes, count):
    rows, columns = value.shape
    parts = value.reshape(count, rows // count, columns)
    return lax.all_to_all(parts, axes, 0, 0, tiled=True).reshape(rows, columns)


def on_device(
    img_emb,
    txt_emb,
    img_ids,
    txt_ids,
    temp_log,
    logit_bias,
    block_in,
    dw_kernel,
    ln_gain,
    ln_bias,
    w_up,
    w_down,
    layer_scale,
    head_gain,
    head_bias,
    w_proj,
):
    blk, txt_all, means = front(
        img_emb,
        txt_emb,
        img_ids.reshape(1, PAIRS),
        txt_ids.reshape(1, PAIRS),
        block_in,
        dw_kernel,
        ln_gain.reshape(1, WIDTH),
        ln_bias.reshape(1, WIDTH),
    )
    texts = swap(txt_all, DP, 16)
    temper = temp_log.reshape(1, 1)
    offset = logit_bias.reshape(1, 1)
    got = {(0, 0): blk}
    kept = []

    def send_on(side, distance, up=True, down=True):
        if up:
            got[NZ - distance, side] = hop(got[(NZ - distance + 1) % NZ, side], "z", NZ, 1)
        if down:
            got[distance, side] = hop(got[distance - 1, side], "z", NZ, -1)

    def tie(keys, *values):
        tied = lax.optimization_barrier((*(got[key] for key in keys), *values))
        got.update(zip(keys, tied))
        return tied[len(keys) :]

    def work(unit):
        return step([got[key] for key in GROUPS[unit]], w_up, texts, temper, offset)

    got[0, 1] = hop(blk, "yhi", 2, 1)
    send_on(0, 1)
    tie([(NZ - 1, 0), (1, 0)])
    send_on(1, 1)
    send_on(0, 2)
    send_on(1, 2)
    send_on(0, 3)
    kept.append(tie([(NZ - 2, 1)], *work(0)))
    send_on(1, 3)
    send_on(0, NZ // 2, down=False)
    kept.append(tie([(3, 1)], *work(1)))
    send_on(1, NZ // 2, up=False)
    kept += [work(unit) for unit in range(2, UNITS)]

    slopes, images, weights, turns, sums, firsts = zip(*kept)
    means_out, total = mean_rows(sums, firsts, w_down)
    means_out, *weights = lax.optimization_barrier((means_out, *weights))
    parts = swap(means_out, FSDP, 16)
    sends = text_parts([got[key] for key in KEYS], weights, images)
    parts, txt_send, txt_keep, img_send, img_keep = lax.optimization_barrier((parts, *sends))
    txt_got = partner(txt_send, "x", 4, 2)
    img_got = hop(img_send, "yhi", 2, 1)
    grads = head(
        parts,
        means,
        layer_scale.reshape(1, WIDTH),
        head_gain.reshape(1, WIDTH),
        head_bias.reshape(1, WIDTH),
        w_proj,
    )
    grads = swap(grads, FSDP, 16)
    sends, keeps = halved((("x", 0), ("z", 0)), (txt_keep, img_keep), (txt_got, img_got))
    grads, *sends = lax.optimization_barrier((grads, *sends))
    gots = (partner(sends[0], "x", 4, 1), partner(sends[1], "z", NZ, 1))
    send, keep = backward(grads, w_down, total, slopes, turns)
    send, *gots = lax.optimization_barrier((send, *gots))
    got_core = hop(send, "core", 2, 1)
    sends, keeps = halved((("ylo", 0), ("z", 1)), keeps, gots)
    gots = (partner(sends[0], "ylo", 2, 1), partner(sends[1], "z", NZ, 2))
    both = join(keep, got_core)
    both, *gots = lax.optimization_barrier((both, *gots))
    sends, keeps = halved((("core", 0), ("z", 2)), keeps, gots)
    w_up_grad, w_down_grad = last(swap(both, ("ylo", "x"), 8))
    w_down_grad = w_down_grad.T
    txt_grad = row_grads((keeps[0], partner(sends[0], "core", 2, 1)), txt_emb, "txt_rows")
    img_grad = row_grads((keeps[1], partner(sends[1], "z", NZ, 4)), img_emb, "img_rows")
    return (img_grad, txt_grad, w_up_grad, w_down_grad)


def solution(mesh):
    split = Mesh(mesh.devices.reshape(2, 4, 2, NZ, 2), ALL)
    in_specs = (
        P(ALL, None),
        P(ALL, None),
        P(ALL),
        P(ALL),
        P(),
        P(),
        P(ALL, None),
        P(),
        P(),
        P(),
        P(None, FSDP),
        P(FSDP, None),
        P(),
        P(),
        P(),
        P(),
    )
    out_specs = (P(ALL, None), P(ALL, None), P(DP, FSDP), P(FSDP, DP))
    return jax.shard_map(
        on_device, mesh=split, in_specs=in_specs, out_specs=out_specs, check_vma=False
    )
```
